128 devices in a mesh: frames: 4 (over x), orient: 32 (over z, y, core).
Axes of the slice: x: 4, y: 4, z: 4, core: 2. Of those that a mesh axis runs over, the one named last changes fastest.
Arguments:
- raw_frames: bfloat16 [256, 4, 64, 16384], P('frames', None, None, 'orient'), may hold values from -6 to 6
- offset_table: bfloat16 [3, 4, 64, 16384], P(None, None, None, 'orient'), may hold values from -3 to 3
- gain_table: bfloat16 [3, 4, 64, 16384], P(None, None, None, 'orient'), may hold values from 0.25 to 4
- gain_section: int32 [4, 64, 16384], P(None, None, 'orient'), may hold values from 0 to 2
- hit_cell: int32 [256, 4], P('frames'), may hold values from 0 to 3, each once within a row
- hit_count: int32 [256], P('frames'), may hold values from 1 to 4, as said below
- train_group: int32 [256], P('frames'), may hold values from 0 to 3, as said below
- tomograms: bfloat16 [8192, 16384], P('orient'), may hold values from 0.2 to 35
Outputs:
- new_tomograms: float32 [8192, 16384], P('orient', 'frames')
- frame_loglik: float32 [1024], P('frames')
The draws below stay inside these ranges and needn't reach their ends.
Inputs may be any that keep to these rules, and one draw needn't show every extreme that they name: `hit_count`: at most 64 live hit frames of the trains of one index of frames go to one group, and in every draw some group receives exactly 64 from every index of frames. `train_group`: each group is given 64 // 4 of the 64 trains of every index of frames.
All inputs are finite; a program needn't handle non-finite values.
Results may differ from the reference program's by a relative error of at most 0.002.
Values may be sent and summed in bfloat16 or wider, within the bound.
A program may use at most 192 MiB of HBM per device.

```python
import math
import jax
import jax.numpy as jnp
from jax import lax

NPIX = 16384
PIXSUB = 64
CELLS = 4
T_DEV = 64
TRAINS = 256
CAP = 64
GROUP_SLOTS = 256
ALL_SLOTS = 1024
ORIENTS = 8192
N_FRAMES = 4


def routing(key):
    base = jax.random.fold_in(key, 911)
    key_perm, key_count, key_full = jax.random.split(base, 3)
    perms = jax.vmap(lambda subkey: jax.random.permutation(subkey, T_DEV))(jax.random.split(key_perm, N_FRAMES))
    groups = (perms // (T_DEV // N_FRAMES)).astype(jnp.int32)
    full_group = jax.random.randint(key_full, (), 0, N_FRAMES)
    counts = jax.random.randint(key_count, (N_FRAMES, T_DEV), 1, CELLS + 1)
    counts = jnp.where(groups == full_group, CELLS, counts).astype(jnp.int32)
    return (counts.reshape(TRAINS), groups.reshape(TRAINS))


def shared_sign(key):
    sign_key = jax.random.fold_in(key, 4242)
    return jnp.where(jax.random.bernoulli(sign_key, 0.5, (NPIX,)), 1.0, -1.0).astype(jnp.float32)


def draw_hit_count(key, part):
    return routing(key)[0]


def draw_train_group(key, part):
    return routing(key)[1]


def draw_raw_frames(key, part):
    key_base = jax.random.fold_in(jax.random.fold_in(key, 313), 0)
    key_strength = jax.random.fold_in(jax.random.fold_in(key, 313), 2)
    key_strong = jax.random.fold_in(jax.random.fold_in(key, 313), 3)
    shape = (TRAINS, CELLS, PIXSUB, NPIX)
    train_index = jnp.arange(TRAINS, dtype=jnp.int32)[:, None, None, None]
    slot_index = jnp.arange(CELLS, dtype=jnp.int32)[None, :, None, None]
    always_strong = (train_index % 8 == 0) & (slot_index == 0)
    strong = jax.random.bernoulli(key_strong, 0.125, (TRAINS, CELLS, 1, 1)) | always_strong
    level_draw = jax.random.randint(key_strength, (TRAINS, CELLS, 1, 1), 1, 5).astype(jnp.float32)
    strength = jnp.where(strong, level_draw, 0.0)
    signal = strength * shared_sign(key)[None, None, None, :]
    values = jax.random.truncated_normal(key_base, -6.0, 6.0, shape, jnp.float32) + signal
    return jnp.clip(values, -6.0, 6.0).astype(jnp.bfloat16)


def draw_tomograms(key, part):
    key_base, key_pixel = jax.random.split(jax.random.fold_in(key, 577))
    shape = (ORIENTS, NPIX)
    logs = 0.6 * jax.random.truncated_normal(key_base, -2.5, 2.5, shape, jnp.float32)
    orient_index = jnp.arange(ORIENTS, dtype=jnp.int32)[:, None]
    aligned_zone = orient_index < ORIENTS // 4
    role = orient_index % 2
    column = jnp.arange(NPIX, dtype=jnp.int32)[None, :]
    chosen = jax.random.randint(key_pixel, (ORIENTS, 1), 0, NPIX)
    dropped = aligned_zone & (role == 1) & (column == chosen)
    aligned = 1.0 + 2.4 * shared_sign(key)[None, :] * jnp.where(dropped, 0.0, 1.0)
    logs = jnp.where(aligned_zone, aligned, logs)
    return jnp.exp(logs).astype(jnp.bfloat16)


def place_ends(result, rng, smallest, high):
    spot = [jax.random.randint(jax.random.fold_in(rng, axis), (), 0, length) for axis, length in enumerate(result.shape)]
    widest = result.shape.index(max(result.shape))
    neighbour = spot[:widest] + [(spot[widest] + 1) % result.shape[widest]] + spot[widest + 1:]
    return result.at[tuple(spot)].set(smallest).at[tuple(neighbour)].set(high)


def level_of(stream_key, extent, cuts, least, largest):
    gain = 1.0
    for axis_at, shards_of in cuts:
        draws = jax.random.uniform(jax.random.fold_in(jax.random.fold_in(stream_key, 6), axis_at), (shards_of,), jnp.float32, least / len(cuts), largest / len(cuts))
        gain = gain * jnp.repeat(jnp.exp(draws), extent[axis_at] // shards_of).reshape((-1,) + (1,) * (len(extent) - 1 - axis_at))
    return gain


def bell_draw(key, dims, deviation, limit, cuts=(), held_as=jnp.bfloat16):
    result = jax.random.normal(key, dims, jnp.float32) * deviation
    if len(cuts) > 0:
        result = level_of(key, dims, cuts, -0.22, 0.18) * result
    return jnp.clip(result, min=-limit, max=limit).astype(held_as)


def setup_inputs(seed: int = 0) -> dict:
    arg_keys = jax.random.split(jax.random.key(seed), 9)
    raw_frames = draw_raw_frames(jax.random.fold_in(arg_keys[8], 71), 0)
    offset_table = bell_draw(arg_keys[1], (3, CELLS, PIXSUB, NPIX), 0.5, 3.0, ((3, 32),))
    gain_table = jnp.clip(jnp.exp(math.log(4.0) - 2.7725887 * jax.random.uniform(arg_keys[2], (3, CELLS, PIXSUB, NPIX), jnp.float32) ** level_of(arg_keys[2], (3, CELLS, PIXSUB, NPIX), ((3, 32),), -0.2, 0.2)), 0.25, 4.0).astype(jnp.bfloat16)
    gain_section = place_ends(jax.random.randint(arg_keys[3], (CELLS, PIXSUB, NPIX), 0, 3), jax.random.fold_in(arg_keys[3], 1), 0, 2).astype(jnp.int32)
    hit_cell = jax.vmap(lambda own: jax.random.permutation(own, CELLS))(jax.random.split(arg_keys[4], TRAINS)).reshape((TRAINS, CELLS)).astype(jnp.int32)
    hit_count = draw_hit_count(jax.random.fold_in(arg_keys[8], 71), 0)
    train_group = draw_train_group(jax.random.fold_in(arg_keys[8], 71), 0)
    tomograms = draw_tomograms(jax.random.fold_in(arg_keys[8], 71), 0)
    return dict(raw_frames=raw_frames, offset_table=offset_table, gain_table=gain_table, gain_section=gain_section, hit_cell=hit_cell, hit_count=hit_count, train_group=train_group, tomograms=tomograms)


smoothing = 0.1

def pick_section(table, section_index):
    return jnp.where(section_index == 0, table[0], jnp.where(section_index == 1, table[1], table[2]))

def reference(raw_frames, offset_table, gain_table, gain_section, hit_cell, hit_count, train_group, tomograms):
    offset_used = pick_section(offset_table, gain_section).astype(jnp.float32)
    gain_used = pick_section(gain_table, gain_section).astype(jnp.float32)

    def bin_train(inputs):
        frame_values, cell_index = inputs
        offsets = jnp.take(offset_used, cell_index, axis=0)
        gains = jnp.take(gain_used, cell_index, axis=0)
        return lax.optimization_barrier(jnp.sum((frame_values.astype(jnp.float32) - offsets) * gains, axis=1)).astype(jnp.bfloat16)
    binned = lax.map(bin_train, (raw_frames, hit_cell))
    counts = hit_count.reshape(N_FRAMES, T_DEV)
    groups = train_group.reshape(N_FRAMES, T_DEV)
    train_order = jnp.arange(T_DEV, dtype=jnp.int32)
    earlier = (groups[:, :, None] == groups[:, None, :]) & (train_order[None, None, :] < train_order[None, :, None])
    preceding = lax.optimization_barrier(jnp.sum(jnp.where(earlier, counts[:, None, :], 0), axis=2)).astype(jnp.int32)
    slot_index = jnp.arange(CELLS, dtype=jnp.int32)
    occupied = slot_index[None, None, :] < counts[:, :, None]
    block_index = jnp.arange(N_FRAMES, dtype=jnp.int32)
    target = groups[:, :, None] * GROUP_SLOTS + block_index[:, None, None] * CAP + preceding[:, :, None] + slot_index[None, None, :]
    target = jnp.where(occupied, target, ALL_SLOTS).astype(jnp.int32).reshape(-1)
    patterns = jnp.zeros((ALL_SLOTS + 1, NPIX), jnp.bfloat16).at[target].set(binned.reshape(-1, NPIX))[:ALL_SLOTS]
    live_rows = jnp.zeros((ALL_SLOTS + 1,), jnp.float32).at[target].set(1.0)[:ALL_SLOTS]
    log_tomo = jnp.log(tomograms.astype(jnp.float32)).astype(jnp.bfloat16)
    scale_factor = 1.2 / math.sqrt(NPIX * PIXSUB)
    scores = scale_factor * lax.dot_general(patterns, log_tomo, (((1,), (1,)), ((), ())), preferred_element_type=jnp.float32)
    highest = lax.optimization_barrier(jnp.max(scores, axis=1))
    weights = jnp.exp(scores - highest[:, None])
    partition = lax.optimization_barrier(jnp.sum(weights, axis=1))
    frame_loglik = (highest + jnp.log(partition)) * live_rows
    responsibility = (weights / partition[:, None] * live_rows[:, None]).astype(jnp.bfloat16)
    numerator = lax.dot_general(responsibility, patterns, (((0,), (0,)), ((), ())), preferred_element_type=jnp.float32)
    denominator = lax.optimization_barrier(jnp.sum(responsibility.astype(jnp.float32), axis=0))
    new_tomograms = (numerator + smoothing * tomograms.astype(jnp.float32)) / (denominator[:, None] + smoothing)
    return (new_tomograms, frame_loglik)
```

```python
import math

import jax
import jax.numpy as jnp
from jax import lax
from jax.experimental import pallas as pl
from jax.experimental.pallas import tpu as pltpu
from jax.sharding import PartitionSpec as P

NPIX = 16384
PIXSUB = 64
SMOOTHING = 0.1
SCALE = 1.2 / math.sqrt(NPIX * PIXSUB)

MESH = pl.DeviceIdType.MESH
F32 = jnp.float32
BF16 = jnp.bfloat16

FX = 4
NT = 64
NC = 4
NF = NT * NC
PB = 512
NR = 256
SLICE = NPIX // FX
KC = 2
FR = NF // 4 // KC
FC = NF // KC


def bin_kernel(cell_ref, count_ref, raw_ref, off_ref, gain_ref, sec_ref, out_ref, gain_s, og_s):
    step = pl.program_id(0)

    @pl.when(step == 0)
    def _():
        for c in range(NC):
            sec = sec_ref[c]
            g = jnp.where(
                sec == 0,
                gain_ref[0, c].astype(F32),
                jnp.where(sec == 1, gain_ref[1, c].astype(F32), gain_ref[2, c].astype(F32)),
            )
            o = jnp.where(
                sec == 0,
                off_ref[0, c].astype(F32),
                jnp.where(sec == 1, off_ref[1, c].astype(F32), off_ref[2, c].astype(F32)),
            )
            gain_s[c] = g
            og_s[c] = jnp.sum(o * g, axis=0, keepdims=True)

    trains = raw_ref.shape[0]
    rows = []
    for i in range(trains):
        t = step * trains + i
        for k in range(NC):
            c = cell_ref[t, k]
            total = jnp.sum(raw_ref[i, k].astype(F32) * gain_s[c], axis=0, keepdims=True)
            live = k < count_ref[t]
            rows.append(jnp.where(live, total - og_s[c], 0.0))
    out_ref[...] = jnp.concatenate(rows, axis=0).astype(BF16)


def bin_frames(raw, off, gain, sec, cell, count):
    bt = 4
    return pl.pallas_call(
        bin_kernel,
        grid=(NT // bt,),
        in_specs=[
            pl.BlockSpec(memory_space=pltpu.SMEM),
            pl.BlockSpec(memory_space=pltpu.SMEM),
            pl.BlockSpec((bt, NC, PIXSUB, PB), lambda i: (i, 0, 0, 0)),
            pl.BlockSpec((3, NC, PIXSUB, PB), lambda i: (0, 0, 0, 0)),
            pl.BlockSpec((3, NC, PIXSUB, PB), lambda i: (0, 0, 0, 0)),
            pl.BlockSpec((NC, PIXSUB, PB), lambda i: (0, 0, 0)),
        ],
        out_specs=pl.BlockSpec((bt * NC, PB), lambda i: (i, 0)),
        out_shape=jax.ShapeDtypeStruct((NF, PB), BF16),
        scratch_shapes=[pltpu.VMEM((NC, PIXSUB, PB), F32), pltpu.VMEM((NC, 1, PB), F32)],
        compiler_params=pltpu.CompilerParams(vmem_limit_bytes=40 << 20),
        name="bin_frames",
    )(cell, count, raw, off, gain, sec)


def comm_kernel(
    bin_ref, tomo_ref, count_ref, group_ref,
    pat_out, resp_out, ll_out,
    pat, tz, tomo, logt, sall, far, near, own, wexp, stat, resp, llsend, llrecv,
    ssem, rsem, lsem,
):
    x = lax.axis_index("frames")
    o = lax.axis_index("orient")
    z = o // 8
    y = (o // 2) % 4
    c = o % 2

    def dev(dx=0, dz=0, dy=0, flip=False):
        cc = 1 - c if flip else c
        return ((x + dx) % 4, ((z + dz) % 4) * 8 + ((y + dy) % 4) * 2 + cc)

    def wrap(v, d):
        return (v + d) % 4

    started = []
    used = [0, 0]

    def send(src, dst, device):
        n = used[0]
        used[0] += 1
        d = pltpu.make_async_remote_copy(
            src_ref=src, dst_ref=dst, send_sem=ssem.at[n], recv_sem=rsem.at[n],
            device_id=device, device_id_type=MESH,
        )
        d.start()
        started.append(d)
        return d

    def local(src, dst):
        n = used[1]
        used[1] += 1
        d = pltpu.make_async_copy(src, dst, lsem.at[n])
        d.start()
        return d

    tomo_copy = local(tomo_ref.at[:, pl.ds(pl.multiple_of(x * SLICE, SLICE), SLICE)], tomo)

    barrier = pltpu.get_barrier_semaphore()
    for i in range(1, 32):
        pl.semaphore_signal(barrier, inc=1, device_id=(x, (o + i) % 32), device_id_type=MESH)
    for d in (1, 2, 3):
        pl.semaphore_signal(barrier, inc=1, device_id=(wrap(x, d), o), device_id_type=MESH)
    pl.semaphore_wait(barrier, 34)

    def piece(k, yy, zz, b0, nb):
        row = pl.multiple_of(zz * FR, FR)
        return pat.at[k, yy, c, pl.ds(b0, nb), pl.ds(row, FR), :]

    def rows_of(k, zz):
        return bin_ref.at[pl.ds(pl.multiple_of(zz * (NF // 4) + k * FR, FR), FR), :]

    zmoves = {}
    for k in range(KC):
        zmoves[k] = [send(rows_of(k, wrap(z, d)), tz.at[k, z], dev(dz=d)) for d in (2, 1, 3)]
        zmoves[k].append(local(rows_of(k, z), tz.at[k, z]))
    xmoves = {}
    for k in range(KC):
        for m in zmoves[k][:3]:
            m.wait_recv()
        zmoves[k][3].wait()
        here = pat.at[k, y, c, x, pl.ds(pl.multiple_of(z * FR, FR), FR), :]
        xmoves[k] = [send(tz.at[k, wrap(x, d)], here, dev(dx=d)) for d in (2, 1, 3)]
        xmoves[k].append(local(tz.at[k, x], here))

    A, B = 0, 2
    yp, ym, zp, zm, pc = dev(dy=1), dev(dy=3), dev(dz=1), dev(dz=3), dev(flip=True)

    def both(ref, device):
        return send(ref, ref, device)

    st = [dict(part=[]) for _ in range(KC)]
    offs = (0, 3, 1, 2)

    def to_partner(k, ref):
        st[k]["part"].append(both(ref, pc))

    def stage1(k):
        for m in xmoves[k][:3]:
            m.wait_recv()
        xmoves[k][3].wait()
        s = st[k]
        ra, rb = piece(k, y, z, A, 2), piece(k, y, z, B, 2)
        s["a1"] = (both(ra, yp), both(ra, ym))
        s["b1"] = (both(rb, zp), both(rb, zm))
        s["a3"] = {0: (both(ra, zp), both(ra, zm))}
        s["b3"] = {0: (both(rb, yp), both(rb, ym))}
        to_partner(k, piece(k, y, z, A, 4))

    def stage2(k):
        s = st[k]
        s["a2"], s["b2"] = [], []
        for i, (fy, fz, half) in enumerate(((yp, zp, 0), (ym, zm, 1))):
            d = offs[i + 1]
            s["a1"][i].wait_recv()
            s["a2"].append(both(piece(k, wrap(y, d), z, A + half, 1), fy))
            r = piece(k, wrap(y, d), z, A, 2)
            s["a3"][i + 1] = (both(r, zp), both(r, zm))
            s["b1"][i].wait_recv()
            s["b2"].append(both(piece(k, y, wrap(z, d), B + half, 1), fz))
            q = piece(k, y, wrap(z, d), B, 2)
            s["b3"][i + 1] = (both(q, yp), both(q, ym))
            to_partner(k, r)
            to_partner(k, q)

    def stage3(k):
        s = st[k]
        for m in s["a2"]:
            m.wait_recv()
        r = piece(k, wrap(y, 2), z, A, 2)
        s["a3"][3] = (both(r, zp), both(r, zm))
        for m in s["b2"]:
            m.wait_recv()
        q = piece(k, y, wrap(z, 2), B, 2)
        s["b3"][3] = (both(q, yp), both(q, ym))
        to_partner(k, r)
        to_partner(k, q)

    def stage4(k, which=(0, 1, 2, 3)):
        s = st[k]
        a4, b4 = s.setdefault("a4", {}), s.setdefault("b4", {})
        for i in which:
            a4[i], b4[i] = [], []
            d = offs[i]
            for h, (fy, fz) in enumerate(((yp, zp), (ym, zm))):
                e = offs[h + 1]
                s["a3"][i][h].wait_recv()
                a4[i].append(both(piece(k, wrap(y, d), wrap(z, e), A + h, 1), fz))
                to_partner(k, piece(k, wrap(y, d), wrap(z, e), A, 2))
                s["b3"][i][h].wait_recv()
                b4[i].append(both(piece(k, wrap(y, e), wrap(z, d), B + h, 1), fy))
                to_partner(k, piece(k, wrap(y, e), wrap(z, d), B, 2))

    def stage5(k):
        s = st[k]
        for i in range(4):
            d = offs[i]
            for m in s["a4"][i]:
                m.wait_recv()
            to_partner(k, piece(k, wrap(y, d), wrap(z, 2), A, 2))
            for m in s["b4"][i]:
                m.wait_recv()
            to_partner(k, piece(k, wrap(y, 2), wrap(z, d), B, 2))

    def stage6(k):
        for m in st[k]["part"]:
            m.wait_recv()
        st[k]["save"] = local(pat.at[k], pat_out.at[k])

    def logs(lo, hi):
        for i in range(lo, hi):
            cols = slice(i * PB, (i + 1) * PB)
            logt[:, cols] = jnp.log(tomo[:, cols].astype(F32)).astype(BF16)

    def dots(k):
        total = None
        for yy in range(4):
            for cc in range(2):
                blk = yy * 2 + cc
                part = lax.dot_general(
                    logt[:, blk * PB:(blk + 1) * PB],
                    pat[k, yy, cc].reshape(FX * FC, PB),
                    (((1,), (1,)), ((), ())),
                    preferred_element_type=F32,
                )
                total = part if total is None else total + part
        sall[k] = total

    HR = NR // 2

    def lanes(d):
        return pl.ds(pl.multiple_of(wrap(x, d) * FC, FC), FC)

    def scatter1(k):
        s = st[k]
        s["far"] = (
            send(sall.at[k, 0:HR, lanes(2)], far.at[k, 0], dev(dx=1)),
            send(sall.at[k, HR:NR, lanes(2)], far.at[k, 1], dev(dx=3)),
        )
        s["near"] = [
            send(sall.at[k, HR:NR, lanes(1)], near.at[k, 0, HR:NR], dev(dx=1)),
            send(sall.at[k, 0:HR, lanes(3)], near.at[k, 1, 0:HR], dev(dx=3)),
        ]

    def scatter2(k):
        s = st[k]
        s["far"][0].wait_recv()
        own[k, 0] = sall[k, 0:HR, lanes(1)] + far[k, 0]
        s["near"].append(send(own.at[k, 0], near.at[k, 0, 0:HR], dev(dx=1)))
        s["far"][1].wait_recv()
        own[k, 1] = sall[k, HR:NR, lanes(3)] + far[k, 1]
        s["near"].append(send(own.at[k, 1], near.at[k, 1, HR:NR], dev(dx=3)))

    def slot_info(k):
        lane = lax.broadcasted_iota(jnp.int32, (NT, FC), 1)
        frame = (lane // FR) * (NF // 4) + k * FR + lane % FR
        train_of = frame // NC
        row = lax.broadcasted_iota(jnp.int32, (NT, FC), 0)
        pick = (row == train_of).astype(F32)
        ahead = (row < train_of).astype(F32)
        count = count_ref[...].astype(F32)
        group = group_ref[...].astype(F32)
        lines = [jnp.where(group == float(g), count, 0.0) for g in range(FX)]
        weights = jnp.concatenate(lines + [count, group, count, group], axis=0)

        def mul(m):
            return lax.dot_general(
                weights, m, (((1,), (0,)), ((), ())),
                preferred_element_type=F32, precision=lax.Precision.HIGHEST,
            )

        here, before = mul(pick), mul(ahead)
        own_group = here[5:6]
        slot = (frame[0:1] % NC).astype(F32)
        live = (slot < here[4:5]).astype(F32)
        place = slot
        for g in range(FX):
            place = place + jnp.where(own_group == float(g), before[g:g + 1], 0.0)
        return live, jnp.where(live > 0.0, place, -1.0), own_group

    def stats1(k):
        s = st[k]
        for m in s["near"]:
            m.wait_recv()
        scores = (sall[k, :, lanes(0)] + near[k, 0] + near[k, 1]) * SCALE
        high = jnp.max(scores, axis=0, keepdims=True)
        weights = jnp.exp(scores - high)
        wexp[k] = weights
        stat[k, o, 0:1, :] = high
        stat[k, o, 1:2, :] = jnp.sum(weights, axis=0, keepdims=True)
        s["stat"] = [send(stat.at[k, o], stat.at[k, o], (x, (o + i) % 32)) for i in range(1, 32)]

    def stats2(k, info):
        s = st[k]
        live, _, _ = info
        mine = stat[k, o, 0:1, :]
        for m in s["stat"]:
            m.wait_recv()
        highs = stat[k, :, 0, :]
        sums = stat[k, :, 1, :]
        highest = jnp.max(highs, axis=0, keepdims=True)
        partition = jnp.sum(sums * jnp.exp(highs - highest), axis=0, keepdims=True)
        factor = jnp.exp(mine - highest) / partition * live
        resp[k, x] = (wexp[k] * factor).astype(BF16)
        s["loglik"] = (highest + jnp.log(partition)) * live
        r = resp.at[k, x]
        s["r1"] = (send(r, r, dev(dx=1)), send(r, r, dev(dx=3)))

    def gather2(k):
        s = st[k]
        s["r1"][0].wait_recv()
        r = resp.at[k, wrap(x, 3), 0:HR]
        s["r2"] = [send(r, r, dev(dx=1))]
        s["r1"][1].wait_recv()
        r = resp.at[k, wrap(x, 1), HR:NR]
        s["r2"].append(send(r, r, dev(dx=3)))

    def send_loglik(infos):
        for g in range(FX):
            total = None
            for k in range(KC):
                _, place, own_group = infos[k]
                slot = lax.broadcasted_iota(jnp.int32, (NF // FX, FC), 0).astype(F32)
                mask = ((slot == place) & (own_group == float(g))).astype(F32)
                line = jnp.broadcast_to(st[k]["loglik"], (8, FC))
                part = lax.dot_general(
                    line, mask, (((1,), (1,)), ((), ())),
                    preferred_element_type=F32, precision=lax.Precision.HIGHEST,
                )
                total = part if total is None else total + part
            llsend[g] = total
        llrecv[x] = llsend[x]
        return [send(llsend.at[wrap(x, d)], llrecv.at[x], dev(dx=d)) for d in (1, 2, 3)]

    stage1(0)
    infos = [slot_info(k) for k in range(KC)]
    tomo_copy.wait()
    logs(0, 2)
    stage2(0)
    stage1(1)
    logs(2, 4)
    stage3(0)
    logs(4, 6)
    stage2(1)
    stage4(0)
    logs(6, 8)
    stage3(1)
    stage5(0)
    stage6(0)
    dots(0)
    scatter1(0)
    stage4(1)
    scatter2(0)
    stage5(1)
    stats1(0)
    stage6(1)
    dots(1)
    scatter1(1)
    stats2(0, infos[0])
    scatter2(1)
    gather2(0)
    stats1(1)
    stats2(1, infos[1])
    ll = send_loglik(infos)
    gather2(1)
    for m in ll:
        m.wait_recv()
    for k in range(KC):
        for m in st[k]["r2"]:
            m.wait_recv()
    saves = [local(resp, resp_out), local(llrecv, ll_out)]
    for d in started:
        d.wait_send()
    for k in range(KC):
        st[k]["save"].wait()
    for d in saves:
        d.wait()


N_REMOTE = 250
N_LOCAL = 16


def exchange(binned, tomograms, count, group):
    return pl.pallas_call(
        comm_kernel,
        in_specs=[
            pl.BlockSpec(memory_space=pltpu.VMEM),
            pl.BlockSpec(memory_space=pl.ANY),
            pl.BlockSpec(memory_space=pltpu.VMEM),
            pl.BlockSpec(memory_space=pltpu.VMEM),
        ],
        out_specs=[pl.BlockSpec(memory_space=pl.ANY)] * 3,
        out_shape=[
            jax.ShapeDtypeStruct((KC, 4, 2, FX, FC, PB), BF16),
            jax.ShapeDtypeStruct((KC, FX, NR, FC), BF16),
            jax.ShapeDtypeStruct((FX, 8, NF // FX), F32),
        ],
        scratch_shapes=[
            pltpu.VMEM((KC, 4, 2, FX, FC, PB), BF16),
            pltpu.VMEM((KC, 4, FR, PB), BF16),
            pltpu.VMEM((NR, SLICE), BF16),
            pltpu.VMEM((NR, SLICE), BF16),
            pltpu.VMEM((KC, NR, FX * FC), F32),
            pltpu.VMEM((KC, 2, NR // 2, FC), F32),
            pltpu.VMEM((KC, 2, NR, FC), F32),
            pltpu.VMEM((KC, 2, NR // 2, FC), F32),
            pltpu.VMEM((KC, NR, FC), F32),
            pltpu.VMEM((KC, 32, 2, FC), F32),
            pltpu.VMEM((KC, FX, NR, FC), BF16),
            pltpu.VMEM((FX, 8, NF // FX), F32),
            pltpu.VMEM((FX, 8, NF // FX), F32),
            pltpu.SemaphoreType.DMA((N_REMOTE,)),
            pltpu.SemaphoreType.DMA((N_REMOTE,)),
            pltpu.SemaphoreType.DMA((N_LOCAL,)),
        ],
        compiler_params=pltpu.CompilerParams(
            collective_id=0, has_side_effects=True, vmem_limit_bytes=48 << 20
        ),
        name="exchange",
    )(binned, tomograms, count, group)


def update_kernel(pat_ref, resp_ref, tomo_ref, ll_ref, out_ref, llo_ref, den_s, tomo, sem):
    step = pl.program_id(0)
    x = lax.axis_index("frames")

    def fetch(i, slot):
        start = pl.multiple_of(x * SLICE + i * PB, PB)
        return pltpu.make_async_copy(tomo_ref.at[:, pl.ds(start, PB)], tomo.at[slot], sem.at[slot])

    @pl.when(step == 0)
    def _():
        fetch(0, 0).start()
        total = None
        for k in range(KC):
            for b in range(FX):
                part = jnp.sum(resp_ref[k, b].astype(F32), axis=1, keepdims=True)
                total = part if total is None else total + part
        den_s[...] = total + SMOOTHING
        for b in range(FX):
            llo_ref[b:b + 1, :] = ll_ref[b, 0:1, :]

    slot = step % 2

    @pl.when(step + 1 < pl.num_programs(0))
    def _():
        fetch(step + 1, 1 - slot).start()

    total = None
    for k in range(KC):
        for b in range(FX):
            part = jnp.dot(resp_ref[k, b], pat_ref[k, 0, 0, b], preferred_element_type=F32)
            total = part if total is None else total + part
    fetch(step, slot).wait()
    out_ref[...] = (total + SMOOTHING * tomo[slot].astype(F32)) / den_s[...]


def update(pat, resp, tomograms, ll):
    return pl.pallas_call(
        update_kernel,
        grid=(8,),
        in_specs=[
            pl.BlockSpec((KC, 1, 1, FX, FC, PB), lambda i: (0, i // 2, i % 2, 0, 0, 0)),
            pl.BlockSpec((KC, FX, NR, FC), lambda i: (0, 0, 0, 0)),
            pl.BlockSpec(memory_space=pl.ANY),
            pl.BlockSpec((FX, 8, NF // FX), lambda i: (0, 0, 0)),
        ],
        out_specs=[
            pl.BlockSpec((NR, PB), lambda i: (0, i)),
            pl.BlockSpec((FX, NF // FX), lambda i: (0, 0)),
        ],
        out_shape=[
            jax.ShapeDtypeStruct((NR, SLICE), F32),
            jax.ShapeDtypeStruct((FX, NF // FX), F32),
        ],
        scratch_shapes=[
            pltpu.VMEM((NR, 1), F32),
            pltpu.VMEM((2, NR, PB), BF16),
            pltpu.SemaphoreType.DMA((2,)),
        ],
        compiler_params=pltpu.CompilerParams(vmem_limit_bytes=40 << 20),
        name="update",
    )(pat, resp, tomograms, ll)


def on_device(
    raw_frames, offset_table, gain_table, gain_section, hit_cell, hit_count, train_group, tomograms
):
    binned = bin_frames(raw_frames, offset_table, gain_table, gain_section, hit_cell, hit_count)
    pat, resp, ll = exchange(
        binned, tomograms, hit_count.reshape(1, NT), train_group.reshape(1, NT)
    )
    new_tomograms, loglik = update(pat, resp, tomograms, ll)
    return new_tomograms, loglik.reshape(NF)


def solution(mesh):
    placed = (
        P("frames", None, None, "orient"),
        P(None, None, None, "orient"),
        P(None, None, None, "orient"),
        P(None, None, "orient"),
        P("frames", None),
        P("frames"),
        P("frames"),
        P("orient", None),
    )
    return jax.shard_map(
        on_device,
        mesh=mesh,
        in_specs=placed,
        out_specs=(P("orient", "frames"), P("frames")),
        check_vma=False,
    )
```

```python
import math

import jax
import jax.numpy as jnp
from jax import lax
from jax.experimental import pallas as pl
from jax.experimental.pallas import tpu as pltpu
from jax.sharding import PartitionSpec as P

NPIX = 16384
PIXSUB = 64
SMOOTHING = 0.1
SCALE = 1.2 / math.sqrt(NPIX * PIXSUB)

MESH = pl.DeviceIdType.MESH
F32 = jnp.float32
BF16 = jnp.bfloat16

FX = 4
NT = 64
NC = 4
NF = NT * NC
PB = 512
NR = 256
SLICE = NPIX // FX
LEVEL = 9
VLIM = 46
KC = 2
FR = NF // 4 // KC
FC = NF // KC


BT = 4
NSTEP = NT // BT
NBUF = 6
PARTS = (2, 1, 3, 0)


def comm_kernel(
    cell_ref, count_s, raw_ref, off_ref, gain_ref, sec_ref, tomo_ref, count_ref, group_ref,
    pat, resp, tomo, llrecv,
    rawb, offb, gainb, secb, gain_s, og_s, acc_s, bin_ref,
    tz, logt, sall, far, near, own, wexp, stat, llsend,
    ssem, rsem, lsem, rawsem,
):
    x = lax.axis_index("frames")
    o = lax.axis_index("orient")
    z = o // 8
    y = (o // 2) % 4
    c = o % 2

    def dev(dx=0, dz=0, dy=0, flip=False):
        cc = 1 - c if flip else c
        return ((x + dx) % 4, ((z + dz) % 4) * 8 + ((y + dy) % 4) * 2 + cc)

    def wrap(v, d):
        return (v + d) % 4

    started = []
    used = [0, 0]

    def send(src, dst, device):
        n = used[0]
        used[0] += 1
        d = pltpu.make_async_remote_copy(
            src_ref=src, dst_ref=dst, send_sem=ssem.at[n], recv_sem=rsem.at[n],
            device_id=device, device_id_type=MESH,
        )
        d.start()
        started.append(d)
        return d

    def local(src, dst):
        n = used[1]
        used[1] += 1
        d = pltpu.make_async_copy(src, dst, lsem.at[n])
        d.start()
        return d

    barrier = pltpu.get_barrier_semaphore()
    for i in range(1, 32):
        pl.semaphore_signal(barrier, inc=1, device_id=(x, (o + i) % 32), device_id_type=MESH)
    for d in (1, 2, 3):
        pl.semaphore_signal(barrier, inc=1, device_id=(wrap(x, d), o), device_id_type=MESH)

    table_copies = [local(sec_ref, secb), local(gain_ref, gainb), local(off_ref, offb)]
    steps = [(k, d, h) for k in range(KC) for d in PARTS for h in range(NSTEP // KC // 4)]

    def fetch(n):
        k, d, h = steps[n]
        first = wrap(z, d) * (NT // 4) + k * (NT // 4 // KC) + h * BT
        return pltpu.make_async_copy(
            raw_ref.at[pl.ds(first, BT)], rawb.at[n % NBUF], rawsem.at[n % NBUF]
        )

    for n in range(NBUF):
        fetch(n).start()
    tomo_copy = local(tomo_ref.at[:, pl.ds(pl.multiple_of(x * SLICE, SLICE), SLICE)], tomo)

    for m in table_copies:
        m.wait()

    def cell_tables(c, carry):
        part = None
        for r in range(PIXSUB // 8):
            rows = slice(r * 8, r * 8 + 8)
            sec = secb[c, rows]

            def chosen(table):
                return jnp.where(
                    sec == 0,
                    table[0, c, rows].astype(F32),
                    jnp.where(sec == 1, table[1, c, rows].astype(F32), table[2, c, rows].astype(F32)),
                )

            g = chosen(gainb)
            gain_s[c, rows] = g
            term = chosen(offb) * g
            part = term if part is None else part + term
        og_s[c] = part
        return carry

    lax.fori_loop(0, NC, cell_tables, 0)

    def bin_step(n):
        k, d, h = steps[n]
        first = wrap(z, d) * (NT // 4) + k * (NT // 4 // KC) + h * BT
        fetch(n).wait()
        buf = n % NBUF

        def train(i, carry):
            count = count_s[first + i]
            for slot in range(NC):
                c = cell_ref[slot, first + i]
                part = None
                for r in range(PIXSUB // 16):
                    v = rawb[buf, i, slot, r * 16:r * 16 + 16].astype(F32)
                    v = v * gain_s[c, r * 16:r * 16 + 16]
                    v = v[0:8] + v[8:16]
                    part = v if part is None else part + v
                part = jnp.where(slot < count, part - og_s[c], 0.0)
                for l in range(PB // 128):
                    row = pl.multiple_of((i * NC + slot) * 8, 8)
                    acc_s[l, pl.ds(row, 8), :] = part[:, l * 128:l * 128 + 128]
            return carry

        lax.fori_loop(0, BT, train, 0)
        row = pl.multiple_of(first * NC, BT * NC)
        for l in range(PB // 128):
            total = None
            for i in range(8):
                part = acc_s[l, pl.ds(i, BT * NC, stride=8), :]
                total = part if total is None else total + part
            bin_ref[pl.ds(row, BT * NC), l * 128:l * 128 + 128] = total.astype(BF16)
        if n + NBUF < NSTEP:
            fetch(n + NBUF).start()

    def piece(k, yy, zz, b0, nb):
        row = pl.multiple_of(zz * FR, FR)
        return pat.at[k, yy, c, pl.ds(b0, nb), pl.ds(row, FR), :]

    def rows_of(k, zz):
        return bin_ref.at[pl.ds(pl.multiple_of(zz * (NF // 4) + k * FR, FR), FR), :]

    zmoves = {k: [] for k in range(KC)}

    def zmove(k, i):
        d = PARTS[i]
        src, dst = rows_of(k, wrap(z, d)), tz.at[k, z]
        zmoves[k].append(local(src, dst) if d == 0 else send(src, dst, dev(dz=d)))

    xmoves = {}

    def xmove(k):
        for m in zmoves[k][:3]:
            m.wait_recv()
        zmoves[k][3].wait()
        here = pat.at[k, y, c, x, pl.ds(pl.multiple_of(z * FR, FR), FR), :]
        xmoves[k] = [send(tz.at[k, wrap(x, d)], here, dev(dx=d)) for d in (2, 1, 3)]
        xmoves[k].append(local(tz.at[k, x], here))

    A, B = 0, 2
    yp, ym, zp, zm, pc = dev(dy=1), dev(dy=3), dev(dz=1), dev(dz=3), dev(flip=True)

    def both(ref, device):
        return send(ref, ref, device)

    st = [dict(part=[]) for _ in range(KC)]
    offs = (0, 3, 1, 2)

    def to_partner(k, ref):
        st[k]["part"].append(both(ref, pc))

    def stage1(k):
        for m in xmoves[k][:3]:
            m.wait_recv()
        xmoves[k][3].wait()
        s = st[k]
        ra, rb = piece(k, y, z, A, 2), piece(k, y, z, B, 2)
        s["a1"] = (both(ra, yp), both(ra, ym))
        s["b1"] = (both(rb, zp), both(rb, zm))
        s["a3"] = {0: (both(ra, zp), both(ra, zm))}
        s["b3"] = {0: (both(rb, yp), both(rb, ym))}
        to_partner(k, piece(k, y, z, A, 4))

    def stage2(k):
        s = st[k]
        s["a2"], s["b2"] = [], []
        for i, (fy, fz, half) in enumerate(((yp, zp, 0), (ym, zm, 1))):
            d = offs[i + 1]
            s["a1"][i].wait_recv()
            s["a2"].append(both(piece(k, wrap(y, d), z, A + half, 1), fy))
            r = piece(k, wrap(y, d), z, A, 2)
            s["a3"][i + 1] = (both(r, zp), both(r, zm))
            s["b1"][i].wait_recv()
            s["b2"].append(both(piece(k, y, wrap(z, d), B + half, 1), fz))
            q = piece(k, y, wrap(z, d), B, 2)
            s["b3"][i + 1] = (both(q, yp), both(q, ym))
            to_partner(k, r)
            to_partner(k, q)

    def stage3(k):
        s = st[k]
        for m in s["a2"]:
            m.wait_recv()
        r = piece(k, wrap(y, 2), z, A, 2)
        s["a3"][3] = (both(r, zp), both(r, zm))
        for m in s["b2"]:
            m.wait_recv()
        q = piece(k, y, wrap(z, 2), B, 2)
        s["b3"][3] = (both(q, yp), both(q, ym))
        to_partner(k, r)
        to_partner(k, q)

    def stage4(k, which=(0, 1, 2, 3)):
        s = st[k]
        a4, b4 = s.setdefault("a4", {}), s.setdefault("b4", {})
        for i in which:
            a4[i], b4[i] = [], []
            d = offs[i]
            for h, (fy, fz) in enumerate(((yp, zp), (ym, zm))):
                e = offs[h + 1]
                s["a3"][i][h].wait_recv()
                a4[i].append(both(piece(k, wrap(y, d), wrap(z, e), A + h, 1), fz))
                to_partner(k, piece(k, wrap(y, d), wrap(z, e), A, 2))
                s["b3"][i][h].wait_recv()
                b4[i].append(both(piece(k, wrap(y, e), wrap(z, d), B + h, 1), fy))
                to_partner(k, piece(k, wrap(y, e), wrap(z, d), B, 2))

    def stage5(k):
        s = st[k]
        for i in range(4):
            d = offs[i]
            for m in s["a4"][i]:
                m.wait_recv()
            to_partner(k, piece(k, wrap(y, d), wrap(z, 2), A, 2))
            for m in s["b4"][i]:
                m.wait_recv()
            to_partner(k, piece(k, wrap(y, 2), wrap(z, d), B, 2))

    def stage6(k):
        for m in st[k]["part"]:
            m.wait_recv()

    def logs(lo, hi):
        for i in range(lo, hi):
            cols = slice(i * PB, (i + 1) * PB)
            logt[:, cols] = jnp.log(tomo[:, cols].astype(F32)).astype(BF16)

    def dots(k):
        total = None
        for yy in range(4):
            for cc in range(2):
                blk = yy * 2 + cc
                part = lax.dot_general(
                    logt[:, blk * PB:(blk + 1) * PB],
                    pat[k, yy, cc].reshape(FX * FC, PB),
                    (((1,), (1,)), ((), ())),
                    preferred_element_type=F32,
                )
                total = part if total is None else total + part
        sall[k] = total

    HR = NR // 2

    def lanes(d):
        return pl.ds(pl.multiple_of(wrap(x, d) * FC, FC), FC)

    def scatter1(k):
        s = st[k]
        s["far"] = (
            send(sall.at[k, 0:HR, lanes(2)], far.at[k, 0], dev(dx=1)),
            send(sall.at[k, HR:NR, lanes(2)], far.at[k, 1], dev(dx=3)),
        )
        s["near"] = [
            send(sall.at[k, HR:NR, lanes(1)], near.at[k, 0, HR:NR], dev(dx=1)),
            send(sall.at[k, 0:HR, lanes(3)], near.at[k, 1, 0:HR], dev(dx=3)),
        ]

    def scatter2(k):
        s = st[k]
        s["far"][0].wait_recv()
        own[k, 0] = sall[k, 0:HR, lanes(1)] + far[k, 0]
        s["near"].append(send(own.at[k, 0], near.at[k, 0, 0:HR], dev(dx=1)))
        s["far"][1].wait_recv()
        own[k, 1] = sall[k, HR:NR, lanes(3)] + far[k, 1]
        s["near"].append(send(own.at[k, 1], near.at[k, 1, HR:NR], dev(dx=3)))

    def slot_info(k):
        lane = lax.broadcasted_iota(jnp.int32, (NT, FC), 1)
        frame = (lane // FR) * (NF // 4) + k * FR + lane % FR
        train_of = frame // NC
        row = lax.broadcasted_iota(jnp.int32, (NT, FC), 0)
        pick = (row == train_of).astype(F32)
        ahead = (row < train_of).astype(F32)
        count = count_ref[...].astype(F32)
        group = group_ref[...].astype(F32)
        lines = [jnp.where(group == float(g), count, 0.0) for g in range(FX)]
        weights = jnp.concatenate(lines + [count, group, count, group], axis=0)

        def mul(m):
            return lax.dot_general(
                weights, m, (((1,), (0,)), ((), ())),
                preferred_element_type=F32, precision=lax.Precision.HIGHEST,
            )

        here, before = mul(pick), mul(ahead)
        own_group = here[5:6]
        slot = (frame[0:1] % NC).astype(F32)
        live = (slot < here[4:5]).astype(F32)
        place = slot
        for g in range(FX):
            place = place + jnp.where(own_group == float(g), before[g:g + 1], 0.0)
        return live, jnp.where(live > 0.0, place, -1.0), own_group

    def stats1(k):
        s = st[k]
        for m in s["near"]:
            m.wait_recv()
        scores = (sall[k, :, lanes(0)] + near[k, 0] + near[k, 1]) * SCALE
        high = jnp.max(scores, axis=0, keepdims=True)
        weights = jnp.exp(scores - high)
        wexp[k] = weights
        stat[k, o, 0:1, :] = high
        stat[k, o, 1:2, :] = jnp.sum(weights, axis=0, keepdims=True)
        s["stat"] = [send(stat.at[k, o], stat.at[k, o], (x, (o + i) % 32)) for i in range(1, 32)]

    def stats2(k, info):
        s = st[k]
        live, _, _ = info
        mine = stat[k, o, 0:1, :]
        for m in s["stat"]:
            m.wait_recv()
        highs = stat[k, :, 0, :]
        sums = stat[k, :, 1, :]
        highest = jnp.max(highs, axis=0, keepdims=True)
        partition = jnp.sum(sums * jnp.exp(highs - highest), axis=0, keepdims=True)
        factor = jnp.exp(mine - highest) / partition * live
        resp[k, :, lanes(0)] = (wexp[k] * factor).astype(BF16)
        s["loglik"] = (highest + jnp.log(partition)) * live
        r = resp.at[k, :, lanes(0)]
        s["r1"] = (send(r, r, dev(dx=1)), send(r, r, dev(dx=3)))

    def gather2(k):
        s = st[k]
        s["r1"][0].wait_recv()
        r = resp.at[k, 0:HR, lanes(3)]
        s["r2"] = [send(r, r, dev(dx=1))]
        s["r1"][1].wait_recv()
        r = resp.at[k, HR:NR, lanes(1)]
        s["r2"].append(send(r, r, dev(dx=3)))

    def send_loglik(infos):
        for g in range(FX):
            total = None
            for k in range(KC):
                _, place, own_group = infos[k]
                slot = lax.broadcasted_iota(jnp.int32, (NF // FX, FC), 0).astype(F32)
                mask = ((slot == place) & (own_group == float(g))).astype(F32)
                line = jnp.broadcast_to(st[k]["loglik"], (8, FC))
                part = lax.dot_general(
                    line, mask, (((1,), (1,)), ((), ())),
                    preferred_element_type=F32, precision=lax.Precision.HIGHEST,
                )
                total = part if total is None else total + part
            llsend[g] = total
        llrecv[x] = llsend[x]
        return [send(llsend.at[wrap(x, d)], llrecv.at[x], dev(dx=d)) for d in (1, 2, 3)]

    def lv(n, f, *a):
        if LEVEL >= n:
            f(*a)

    per = NSTEP // KC // 4
    for n in range(NSTEP // 2):
        bin_step(n)
        if n == per:
            pl.semaphore_wait(barrier, 34)
        if n >= per and n % per == per - 1:
            lv(1, zmove, 0, n // per - 1)
    bin_step(NSTEP // 2)
    lv(1, zmove, 0, 3)
    infos = [slot_info(k) for k in range(KC)]
    for n in range(NSTEP // 2 + 1, NSTEP):
        bin_step(n)
        m = n - NSTEP // 2
        if m >= per and m % per == per - 1:
            lv(1, zmove, 1, m // per - 1)
        if m == 3:
            lv(1, xmove, 0)
        if m == 6:
            lv(2, stage1, 0)
    tomo_copy.wait()
    lv(3, logs, 0, 1)
    lv(1, zmove, 1, 3)
    lv(2, stage2, 0)
    lv(3, logs, 1, 3)
    lv(1, xmove, 1)
    lv(2, stage3, 0)
    lv(3, logs, 3, 5)
    lv(2, stage1, 1)
    lv(2, stage4, 0)
    lv(3, logs, 5, 6)
    lv(2, stage2, 1)
    lv(3, logs, 6, 7)
    lv(2, stage5, 0)
    lv(2, stage3, 1)
    lv(3, logs, 7, 8)
    lv(2, stage6, 0)
    lv(4, dots, 0)
    lv(5, scatter1, 0)
    lv(2, stage4, 1)
    lv(5, scatter2, 0)
    lv(2, stage5, 1)
    lv(6, stats1, 0)
    lv(2, stage6, 1)
    lv(4, dots, 1)
    lv(5, scatter1, 1)
    lv(6, stats2, 0, infos[0])
    lv(5, scatter2, 1)
    lv(7, gather2, 0)
    lv(6, stats1, 1)
    lv(6, stats2, 1, infos[1])
    if LEVEL >= 7:
        ll = send_loglik(infos)
        gather2(1)
        for m in ll:
            m.wait_recv()
    for k in range(KC):
        if LEVEL == 1:
            for m in xmoves[k][:3]:
                m.wait_recv()
            xmoves[k][3].wait()
        if LEVEL == 5:
            for m in st[k]["near"]:
                m.wait_recv()
        if LEVEL == 6:
            for m in st[k]["r1"]:
                m.wait_recv()
        for m in st[k].get("r2", []):
            m.wait_recv()
    for d in started:
        d.wait_send()


N_REMOTE = 250
N_LOCAL = 16


def exchange(raw, off, gain, sec, cell, tomograms, count, group):
    vmem = pl.BlockSpec(memory_space=pltpu.VMEM)
    smem = pl.BlockSpec(memory_space=pltpu.SMEM)
    any_ = pl.BlockSpec(memory_space=pltpu.HBM)
    return pl.pallas_call(
        comm_kernel,
        in_specs=[smem, smem, any_, any_, any_, any_, any_, vmem, vmem],
        out_specs=[vmem] * 4,
        out_shape=[
            pltpu.VMEM((KC, 4, 2, FX, FC, PB), BF16),
            pltpu.VMEM((KC, NR, FX * FC), BF16),
            pltpu.VMEM((NR, SLICE), BF16),
            pltpu.VMEM((FX, 8, NF // FX), F32),
        ],
        scratch_shapes=[
            pltpu.VMEM((NBUF, BT, NC, PIXSUB, PB), BF16),
            pltpu.VMEM((3, NC, PIXSUB, PB), BF16),
            pltpu.VMEM((3, NC, PIXSUB, PB), BF16),
            pltpu.VMEM((NC, PIXSUB, PB), jnp.int32),
            pltpu.VMEM((NC, PIXSUB, PB), F32),
            pltpu.VMEM((NC, 8, PB), F32),
            pltpu.VMEM((PB // 128, BT * NC * 8, 128), F32),
            pltpu.VMEM((NF, PB), BF16),
            pltpu.VMEM((KC, 4, FR, PB), BF16),
            pltpu.VMEM((NR, SLICE), BF16),
            pltpu.VMEM((KC, NR, FX * FC), F32),
            pltpu.VMEM((KC, 2, NR // 2, FC), F32),
            pltpu.VMEM((KC, 2, NR, FC), F32),
            pltpu.VMEM((KC, 2, NR // 2, FC), F32),
            pltpu.VMEM((KC, NR, FC), F32),
            pltpu.VMEM((KC, 32, 2, FC), F32),
            pltpu.VMEM((FX, 8, NF // FX), F32),
            pltpu.SemaphoreType.DMA((N_REMOTE,)),
            pltpu.SemaphoreType.DMA((N_REMOTE,)),
            pltpu.SemaphoreType.DMA((N_LOCAL,)),
            pltpu.SemaphoreType.DMA((NBUF,)),
        ],
        compiler_params=pltpu.CompilerParams(
            collective_id=0, has_side_effects=True, vmem_limit_bytes=VLIM << 20
        ),
        name="exchange",
    )(cell.T, count, raw, off, gain, sec, tomograms, count.reshape(1, NT), group.reshape(1, NT))


def update_kernel(pat_ref, resp_ref, tomo_ref, ll_ref, out_ref, llo_ref, inv_s):
    step = pl.program_id(0)

    @pl.when(step == 0)
    def _():
        total = None
        for k in range(KC):
            part = jnp.sum(resp_ref[k].astype(F32), axis=1, keepdims=True)
            total = part if total is None else total + part
        inv_s[...] = 1.0 / (total + SMOOTHING)
        llo_ref[...] = jnp.concatenate([ll_ref[b, 0:1, :] for b in range(FX)], axis=1)

    total = None
    for k in range(KC):
        part = jnp.dot(
            resp_ref[k], pat_ref[k, step // 2, step % 2].reshape(FX * FC, PB),
            preferred_element_type=F32,
        )
        total = part if total is None else total + part
    columns = pl.ds(pl.multiple_of(step * PB, PB), PB)
    out_ref[...] = (total + SMOOTHING * tomo_ref[:, columns].astype(F32)) * inv_s[...]


def update(pat, resp, tomo, ll):
    vmem = pl.BlockSpec(memory_space=pltpu.VMEM)
    return pl.pallas_call(
        update_kernel,
        grid=(8,),
        in_specs=[vmem] * 4,
        out_specs=[
            pl.BlockSpec((NR, PB), lambda i: (0, i)),
            pl.BlockSpec((1, NF), lambda i: (0, 0)),
        ],
        out_shape=[
            jax.ShapeDtypeStruct((NR, SLICE), F32),
            jax.ShapeDtypeStruct((1, NF), F32),
        ],
        scratch_shapes=[pltpu.VMEM((NR, 1), F32)],
        compiler_params=pltpu.CompilerParams(vmem_limit_bytes=32 << 20),
        name="update",
    )(pat, resp, tomo, ll)


def on_device(
    raw_frames, offset_table, gain_table, gain_section, hit_cell, hit_count, train_group, tomograms
):
    pat, resp, tomo, ll = exchange(
        raw_frames, offset_table, gain_table, gain_section, hit_cell, tomograms,
        hit_count, train_group,
    )
    new_tomograms, loglik = update(pat, resp, tomo, ll)
    return new_tomograms, loglik.reshape(NF)


def solution(mesh):
    placed = (
        P("frames", None, None, "orient"),
        P(None, None, None, "orient"),
        P(None, None, None, "orient"),
        P(None, None, "orient"),
        P("frames", None),
        P("frames"),
        P("frames"),
        P("orient", None),
    )
    return jax.shard_map(
        on_device,
        mesh=mesh,
        in_specs=placed,
        out_specs=(P("orient", "frames"), P("frames")),
        check_vma=False,
    )
```

```python
import functools
import math

import jax
import jax.numpy as jnp
from jax import lax
from jax.experimental import pallas as pl
from jax.experimental.pallas import tpu as pltpu
from jax.sharding import PartitionSpec as P

NPIX = 16384
PIXSUB = 64
SMOOTHING = 0.1
SCALE = 1.2 / math.sqrt(NPIX * PIXSUB)

MESH = pl.DeviceIdType.MESH
F32 = jnp.float32
BF16 = jnp.bfloat16

FX = 4
NT = 64
NC = 4
NF = NT * NC
PB = 512
NR = 256
SLICE = NPIX // FX
KC = 2
QC = 2
NQ = KC * QC
FR = NF // 4 // NQ
FC = NF // KC


BT = 4
NSTEP = NT // BT
NBUF = 6
PARTS = (2, 1, 3, 0)


def comm_kernel(
    cell_in, count_in, raw_ref, off_ref, gain_ref, sec_ref, tomo_ref, count_row, group_row,
    pat, resp, tomo, num, llrecv,
    rawb, offb, gainb, secb, gain_s, og_s, acc_s, bin_ref,
    tz, logt, sall, far, near, own, wexp, high_s, staty, statz, llsend,
    cell_ref, count_s, count_ref, group_ref,
    ssem, rsem, lsem, rawsem,
):
    x = lax.axis_index("frames")
    o = lax.axis_index("orient")
    z = o // 8
    y = (o // 2) % 4
    c = o % 2

    def dev(dx=0, dz=0, dy=0, flip=False):
        cc = 1 - c if flip else c
        return ((x + dx) % 4, ((z + dz) % 4) * 8 + ((y + dy) % 4) * 2 + cc)

    def wrap(v, d):
        return (v + d) % 4

    started = []
    used = [0, 0]

    group_of, groups, sem_of = {}, {}, {}

    def group(name, keys, ref):
        groups[name] = (tuple(keys), ref)
        for key in keys:
            group_of[key] = name

    def remote(key, src, dst, device):
        n = used[0]
        used[0] += 1
        if n >= N_SEND:
            started[n - N_SEND].wait_send()
        sem = sem_of.setdefault(group_of.get(key, key), len(sem_of))
        d = pltpu.make_async_remote_copy(
            src_ref=src, dst_ref=dst, send_sem=ssem.at[n % N_SEND], recv_sem=rsem.at[sem],
            device_id=device, device_id_type=MESH,
        )
        d.start()
        started.append(d)
        arrivals[key] = d

    def await_arrival(name):
        if name in groups:
            keys, ref = groups[name]
            assert all(key in arrivals for key in keys)
            pltpu.make_async_copy(ref, ref, rsem.at[sem_of[name]]).wait()
        else:
            arrivals[name].wait_recv()

    def local(src, dst):
        n = used[1]
        used[1] += 1
        d = pltpu.make_async_copy(src, dst, lsem.at[n])
        d.start()
        return d

    barrier = pltpu.get_barrier_semaphore()
    peers = [dev(dx=d) for d in (1, 2, 3)] + [dev(dz=d) for d in (1, 2, 3)]
    peers += [dev(dy=d, flip=f) for d in range(4) for f in (False, True) if d or f]
    for p in peers:
        pl.semaphore_signal(barrier, inc=1, device_id=p, device_id_type=MESH)

    small_copies = [
        local(cell_in, cell_ref), local(count_in, count_s),
        local(count_row, count_ref), local(group_row, group_ref),
    ]
    table_copies = [local(sec_ref, secb), local(gain_ref, gainb), local(off_ref, offb)]
    steps = [(q, d, h) for q in range(NQ) for d in PARTS for h in range(NSTEP // NQ // 4)]

    def first_train(n):
        q, d, h = steps[n]
        return wrap(z, d) * (NT // 4) + q * (NT // 4 // NQ) + h * BT

    def fetch(n):
        first = first_train(n)
        return pltpu.make_async_copy(
            raw_ref.at[pl.ds(first, BT)], rawb.at[n % NBUF], rawsem.at[n % NBUF]
        )

    for n in range(NBUF):
        fetch(n).start()

    for m in table_copies + small_copies:
        m.wait()

    def cell_tables(c, carry):
        part = None
        for r in range(PIXSUB // 8):
            rows = slice(r * 8, r * 8 + 8)
            sec = secb[c, rows]

            def chosen(table):
                return jnp.where(
                    sec == 0,
                    table[0, c, rows].astype(F32),
                    jnp.where(sec == 1, table[1, c, rows].astype(F32), table[2, c, rows].astype(F32)),
                )

            g = chosen(gainb)
            gain_s[c, rows] = g
            term = chosen(offb) * g
            part = term if part is None else part + term
        og_s[c] = part
        return carry

    lax.fori_loop(0, NC, cell_tables, 0)

    def bin_step(n):
        first = first_train(n)
        fetch(n).wait()
        if n == NSTEP - NBUF:
            columns = pl.ds(pl.multiple_of(x * SLICE, SLICE), SLICE)
            kept["tomo"] = local(tomo_ref.at[:, columns], tomo)
        buf = n % NBUF

        def train(i, carry):
            count = count_s[first + i]
            for slot in range(NC):
                c = cell_ref[slot, first + i]
                part = None
                for r in range(PIXSUB // 16):
                    v = rawb[buf, i, slot, r * 16:r * 16 + 16].astype(F32)
                    v = v * gain_s[c, r * 16:r * 16 + 16]
                    v = v[0:8] + v[8:16]
                    part = v if part is None else part + v
                part = jnp.where(slot < count, part - og_s[c], 0.0)
                for l in range(PB // 128):
                    row = pl.multiple_of((i * NC + slot) * 8, 8)
                    acc_s[l, pl.ds(row, 8), :] = part[:, l * 128:l * 128 + 128]
            return carry

        lax.fori_loop(0, BT, train, 0)
        row = pl.multiple_of(first * NC, BT * NC)
        for l in range(PB // 128):
            total = None
            for i in range(8):
                part = acc_s[l, pl.ds(i, BT * NC, stride=8), :]
                total = part if total is None else total + part
            bin_ref[pl.ds(row, BT * NC), l * 128:l * 128 + 128] = total.astype(BF16)
        if n + NBUF < NSTEP:
            fetch(n + NBUF).start()

    tasks = []
    arrivals = {}

    def task(name, fn=None, waits=(), after=(), sends=(), cost=0.0, prio=0):
        tasks.append((name, fn, tuple(waits), tuple(after), tuple(sends), cost, prio))

    def piece(q, yy, zz, b0, nb):
        row = pl.multiple_of((q % QC) * 4 * FR + zz * FR, FR)
        return pat.at[q // QC, yy, c, pl.ds(b0, nb), pl.ds(row, FR), :]

    def rows_of(q, zz):
        return bin_ref.at[pl.ds(pl.multiple_of(zz * (NF // 4) + q * FR, FR), FR), :]

    LINKS = {
        "x+": dev(dx=1), "x-": dev(dx=3), "x2": dev(dx=2), "z+": dev(dz=1), "z-": dev(dz=3),
        "z2": dev(dz=2), "y+": dev(dy=1), "y-": dev(dy=3), "pc": dev(flip=True),
    }

    def snd(key, src, dst, link, kb):
        return (key, src, dst, link, kb)

    def same(key, ref, link, kb):
        return (key, ref, ref, link, kb)

    per = NSTEP // NQ // 4
    kept = {}

    def wait_barrier():
        pl.semaphore_wait(barrier, len(peers))

    task("bar", wait_barrier, after=["bin%d" % (per - 1)], cost=0.1)
    PK = FR * PB * 2 / 1024.0
    for n in range(NSTEP):
        task("bin%d" % n, functools.partial(bin_step, n), after=["bin%d" % (n - 1)] if n else [], cost=0.42)

    def keep_local(name, src, dst):
        kept[name] = local(src, dst)

    for q in range(NQ):
        for i, d in enumerate(PARTS):
            last = min((q * 4 + i + 1) * per, NSTEP - 1)
            after = ["bin%d" % last, "bar"]
            src, dst = rows_of(q, wrap(z, d)), tz.at[q, z]
            name = "z%d.%d" % (q, d)
            if d == 0:
                task(name, functools.partial(keep_local, name, src, dst), after=after, cost=0.03, prio=3)
            else:
                link = ("", "z+", "z2", "z-")[d]
                task(name, after=after, sends=[snd(name, src, dst, link, PK)], prio=3)

        here = pat.at[
            q // QC, y, c, x, pl.ds(pl.multiple_of((q % QC) * 4 * FR + z * FR, FR), FR), :
        ]

        def start_own(q=q, here=here):
            kept["z%d.0" % q].wait()
            kept["x%d" % q] = local(tz.at[q, x], here)

        group("zg%d" % q, ["z%d.%d" % (q, d) for d in (2, 1, 3)], tz.at[q, 0:3])
        group("xg%d" % q, ["x%d.%d" % (q, d) for d in (2, 1, 3)], tz.at[q, 0:3])
        task(
            "x%d" % q, start_own, waits=["zg%d" % q], after=["z%d.0" % q],
            sends=[
                snd("x%d.%d" % (q, d), tz.at[q, wrap(x, d)], here, ("", "x+", "x2", "x-")[d], PK)
                for d in (2, 1, 3)
            ], prio=3, cost=0.03,
        )

    A, B = 0, 2
    offs = (0, 3, 1, 2)

    def cast(q):
        def nm(t, *ids):
            return t + str(q) + "".join("." + str(i) for i in ids)

        ra, rb = piece(q, y, z, A, 2), piece(q, y, z, B, 2)
        task(
            nm("s"), lambda: kept["x%d" % q].wait(), waits=["xg%d" % q],
            after=["x%d" % q],
            sends=[
                same(nm("a1", 0), ra, "y+", 2 * PK), same(nm("a1", 1), ra, "y-", 2 * PK),
                same(nm("b1", 0), rb, "z+", 2 * PK), same(nm("b1", 1), rb, "z-", 2 * PK),
                same(nm("a3", 0, 0), ra, "z+", 2 * PK), same(nm("a3", 0, 1), ra, "z-", 2 * PK),
                same(nm("b3", 0, 0), rb, "y+", 2 * PK), same(nm("b3", 0, 1), rb, "y-", 2 * PK),
                same(nm("p", 0), piece(q, y, z, A, 4), "pc", 4 * PK),
            ], prio=2,
        )
        for h, (fy, fz) in enumerate((("y+", "z+"), ("y-", "z-"))):
            d = offs[h + 1]
            r, p = piece(q, wrap(y, d), z, A, 2), piece(q, wrap(y, d), z, A + h, 1)
            task(
                nm("ha", h), waits=[nm("a1", h)],
                sends=[
                    same(nm("a2", h), p, fy, PK),
                    same(nm("a3", h + 1, 0), r, "z+", 2 * PK), same(nm("a3", h + 1, 1), r, "z-", 2 * PK),
                    same(nm("p", 1 + h), r, "pc", 2 * PK),
                ], prio=2,
            )
            r, p = piece(q, y, wrap(z, d), B, 2), piece(q, y, wrap(z, d), B + h, 1)
            task(
                nm("hb", h), waits=[nm("b1", h)],
                sends=[
                    same(nm("b2", h), p, fz, PK),
                    same(nm("b3", h + 1, 0), r, "y+", 2 * PK), same(nm("b3", h + 1, 1), r, "y-", 2 * PK),
                    same(nm("p", 3 + h), r, "pc", 2 * PK),
                ], prio=2,
            )
        r = piece(q, wrap(y, 2), z, A, 2)
        group(nm("a2"), [nm("a2", 0), nm("a2", 1)], r)
        task(
            nm("ia"), waits=[nm("a2")],
            sends=[
                same(nm("a3", 3, 0), r, "z+", 2 * PK), same(nm("a3", 3, 1), r, "z-", 2 * PK),
                same(nm("p", 5), r, "pc", 2 * PK),
            ], prio=2,
        )
        r = piece(q, y, wrap(z, 2), B, 2)
        group(nm("b2"), [nm("b2", 0), nm("b2", 1)], r)
        task(
            nm("ib"), waits=[nm("b2")],
            sends=[
                same(nm("b3", 3, 0), r, "y+", 2 * PK), same(nm("b3", 3, 1), r, "y-", 2 * PK),
                same(nm("p", 6), r, "pc", 2 * PK),
            ], prio=2,
        )

        def column(zz):
            row = pl.multiple_of((q % QC) * 4 * FR + zz * FR, FR)
            return pat.at[q // QC, :, c, pl.ds(A, 2), pl.ds(row, FR), :]

        def line(yy):
            return pat.at[q // QC, yy, c, pl.ds(B, 2), pl.ds((q % QC) * 4 * FR, 4 * FR), :]

        for h, (fy, fz) in enumerate((("y+", "z+"), ("y-", "z-"))):
            e = offs[h + 1]
            for i in range(4):
                d = offs[i]
                task(
                    nm("ja", i, h), waits=[nm("a3", i, h)],
                    sends=[same(nm("a4", i, h), piece(q, wrap(y, d), wrap(z, e), A + h, 1), fz, PK)],
                    prio=2,
                )
                task(
                    nm("jb", i, h), waits=[nm("b3", i, h)],
                    sends=[same(nm("b4", i, h), piece(q, wrap(y, e), wrap(z, d), B + h, 1), fy, PK)],
                    prio=2,
                )
            task(
                nm("ka", h), after=[nm("ja", i, h) for i in range(4)],
                sends=[same(nm("p", 7 + h), column(wrap(z, e)), "pc", 8 * PK)], prio=1,
            )
            task(
                nm("kb", h), after=[nm("jb", i, h) for i in range(4)],
                sends=[same(nm("p", 9 + h), line(wrap(y, e)), "pc", 8 * PK)], prio=1,
            )
        group(nm("a4"), [nm("a4", i, h) for i in range(4) for h in range(2)], column(wrap(z, 2)))
        group(nm("b4"), [nm("b4", i, h) for i in range(4) for h in range(2)], line(wrap(y, 2)))
        rows = pl.ds((q % QC) * 4 * FR, 4 * FR)
        group(nm("p"), [nm("p", i) for i in range(13)], pat.at[q // QC, :, 1 - c, :, rows, :])
        task(
            nm("la"), waits=[nm("a4")],
            sends=[same(nm("p", 11), column(wrap(z, 2)), "pc", 8 * PK)], prio=2,
        )
        task(
            nm("lb"), waits=[nm("b4")],
            sends=[same(nm("p", 12), line(wrap(y, 2)), "pc", 8 * PK)], prio=2,
        )
        task(nm("done"), waits=[nm("p")], after=[nm("la"), nm("lb")], prio=5)

    for q in range(NQ):
        cast(q)

    def log_block(i):
        if i == 0:
            kept["tomo"].wait()
        cols = slice(i * PB, (i + 1) * PB)
        logt[:, cols] = jnp.log(tomo[:, cols].astype(F32)).astype(BF16)

    for i in range(8):
        task(
            "log%d" % i, functools.partial(log_block, i),
            after=["log%d" % (i - 1)] if i else ["bin%d" % (NSTEP - 1)], cost=0.35,
        )

    HR = NR // 2

    def lanes(d):
        return pl.ds(pl.multiple_of(wrap(x, d) * FC, FC), FC)

    infos = {}

    def slot_info(k):
        lane = lax.broadcasted_iota(jnp.int32, (NT, FC), 1)
        frame = (lane % (4 * FR)) // FR * (NF // 4) + (k * QC + lane // (4 * FR)) * FR + lane % FR
        train_of = frame // NC
        row = lax.broadcasted_iota(jnp.int32, (NT, FC), 0)
        pick = (row == train_of).astype(F32)
        ahead = (row < train_of).astype(F32)
        count = count_ref[...].astype(F32)
        group = group_ref[...].astype(F32)
        by_group = [jnp.where(group == float(g), count, 0.0) for g in range(FX)]
        weights = jnp.concatenate(by_group + [count, group, count, group], axis=0)

        def mul(m):
            return lax.dot_general(
                weights, m, (((1,), (0,)), ((), ())),
                preferred_element_type=F32, precision=lax.Precision.HIGHEST,
            )

        here, before = mul(pick), mul(ahead)
        own_group = here[5:6]
        slot = (frame[0:1] % NC).astype(F32)
        live = (slot < here[4:5]).astype(F32)
        place = slot
        for g in range(FX):
            place = place + jnp.where(own_group == float(g), before[g:g + 1], 0.0)
        infos[k] = (live, jnp.where(live > 0.0, place, -1.0), own_group)

    loglik = {}

    def scores_chain(k):
        def nm(t, *ids):
            return t + "k" + str(k) + "".join("." + str(i) for i in ids)

        task(nm("info"), functools.partial(slot_info, k), after=["bin%d" % (NSTEP - 1)], cost=0.5, prio=-1)

        def dots():
            total = None
            for yy in range(4):
                for cc in range(2):
                    blk = yy * 2 + cc
                    part = lax.dot_general(
                        logt[:, blk * PB:(blk + 1) * PB],
                        pat[k, yy, cc].reshape(FX * FC, PB),
                        (((1,), (1,)), ((), ())),
                        preferred_element_type=F32,
                    )
                    total = part if total is None else total + part
            sall[k] = total

        SK = HR * FC * 4 / 1024.0
        task(
            nm("dots"), dots, after=["done%d" % (k * QC + i) for i in range(QC)] + ["log7"], cost=0.8, prio=1,
            sends=[
                snd(nm("far", 0), sall.at[k, 0:HR, lanes(2)], far.at[k, 0], "x+", SK),
                snd(nm("far", 1), sall.at[k, HR:NR, lanes(2)], far.at[k, 1], "x-", SK),
                snd(nm("near", 0), sall.at[k, HR:NR, lanes(1)], near.at[k, 0, HR:NR], "x+", SK),
                snd(nm("near", 1), sall.at[k, 0:HR, lanes(3)], near.at[k, 1, 0:HR], "x-", SK),
            ],
        )

        def add(h):
            rows, d = ((slice(0, HR), 1), (slice(HR, NR), 3))[h]
            own[k, h] = sall[k, rows, lanes(d)] + far[k, h]

        task(
            nm("add", 0), functools.partial(add, 0), waits=[nm("far", 0)], cost=0.05, prio=2,
            sends=[snd(nm("near", 2), own.at[k, 0], near.at[k, 0, 0:HR], "x+", SK)],
        )
        task(
            nm("add", 1), functools.partial(add, 1), waits=[nm("far", 1)], cost=0.05, prio=2,
            sends=[snd(nm("near", 3), own.at[k, 1], near.at[k, 1, HR:NR], "x-", SK)],
        )

        def stats1():
            scores = (sall[k, :, lanes(0)] + near[k, 0] + near[k, 1]) * SCALE
            high = jnp.max(scores, axis=0, keepdims=True)
            weights = jnp.exp(scores - high)
            wexp[k] = weights
            mine = staty.at[k, y * 2 + c]
            mine[0:1, :] = high
            mine[1:2, :] = jnp.sum(weights, axis=0, keepdims=True)
            high_s[k] = high

        group(nm("near"), [nm("near", i) for i in range(4)], near.at[k])
        group(nm("sy"), [nm("sy", d, f) for d in range(4) for f in range(2) if d or f], staty.at[k, 0:7])
        group(nm("sz"), [nm("sz", d) for d in (1, 2, 3)], statz.at[k, 0:3])
        group(nm("r2"), [nm("r2", 0), nm("r2", 1)], resp.at[k, :, lanes(2)])
        mine = staty.at[k, y * 2 + c]
        task(
            nm("st1"), stats1, waits=[nm("near")], cost=0.3, prio=2,
            sends=[
                snd(nm("sy", d, f), mine, mine, dev(dy=d, flip=bool(f)), 1.0)
                for d in range(4) for f in range(2) if d or f
            ],
        )

        def merge(ref):
            highs, sums = ref[k, :, 0, :], ref[k, :, 1, :]
            high = jnp.max(highs, axis=0, keepdims=True)
            return high, jnp.sum(sums * jnp.exp(highs - high), axis=0, keepdims=True)

        def stats2():
            high, total = merge(staty)
            mine = statz.at[k, z]
            mine[0:1, :] = high
            mine[1:2, :] = total

        minez = statz.at[k, z]
        task(
            nm("st2"), stats2, cost=0.1, prio=2,
            waits=[nm("sy")],
            sends=[snd(nm("sz", d), minez, minez, dev(dz=d), 1.0) for d in (2, 1, 3)],
        )

        def stats3():
            live = infos[k][0]
            highest, partition = merge(statz)
            factor = jnp.exp(high_s[k] - highest) / partition * live
            resp[k, :, lanes(0)] = (wexp[k] * factor).astype(BF16)
            loglik[k] = (highest + jnp.log(partition)) * live

        RK = NR * FC * 2 / 1024.0
        r = resp.at[k, :, lanes(0)]
        task(
            nm("st3"), stats3, waits=[nm("sz")], after=[nm("info")], cost=0.3, prio=2,
            sends=[same(nm("r1", 0), r, "x+", RK), same(nm("r1", 1), r, "x-", RK)],
        )
        task(
            nm("g", 0), waits=[nm("r1", 0)], prio=2,
            sends=[same(nm("r2", 0), resp.at[k, 0:HR, lanes(3)], "x+", RK / 2)],
        )
        task(
            nm("g", 1), waits=[nm("r1", 1)], prio=2,
            sends=[same(nm("r2", 1), resp.at[k, HR:NR, lanes(1)], "x-", RK / 2)],
        )

    for k in range(KC):
        scores_chain(k)

    def place_loglik():
        for g in range(FX):
            total = None
            for k in range(KC):
                _, place, own_group = infos[k]
                slot = lax.broadcasted_iota(jnp.int32, (NF // FX, FC), 0).astype(F32)
                mask = ((slot == place) & (own_group == float(g))).astype(F32)
                part = lax.dot_general(
                    jnp.broadcast_to(loglik[k], (8, FC)), mask, (((1,), (1,)), ((), ())),
                    preferred_element_type=F32, precision=lax.Precision.HIGHEST,
                )
                total = part if total is None else total + part
            llsend[g] = total
        llrecv[x] = llsend[x]

    task(
        "ll", place_loglik, after=["st3k%d" % k for k in range(KC)], cost=0.4, prio=1,
        sends=[snd("ll.%d" % d, llsend.at[wrap(x, d)], llrecv.at[x], dev(dx=d), 2.0) for d in (2, 1, 3)],
    )
    group("llg", ["ll.%d" % d for d in (1, 2, 3)], llrecv.at[0:3])

    def part_of_numerator(i):
        total = None
        for k in range(KC - 1):
            part = jnp.dot(
                resp[k], pat[k, i // 2, i % 2].reshape(FX * FC, PB), preferred_element_type=F32
            )
            total = part if total is None else total + part
        num[:, i * PB:(i + 1) * PB] = total

    for i in range(8):
        before = ["num%d" % (i - 1)] if i else ["gk%d.%d" % (KC - 2, h) for h in range(2)]
        waits = [] if i else ["r2k%d" % k for k in range(KC - 1)]
        task("num%d" % i, functools.partial(part_of_numerator, i), waits=waits, after=before, cost=0.35)
    task(
        "end", waits=["llg", "r2k%d" % (KC - 1)],
        after=["gk%d.%d" % (KC - 1, h) for h in range(2)] + ["num7"],
    )

    for name, fn, waits, _, sends, _, _ in in_order(tasks, groups):
        for w in waits:
            await_arrival(w)
        if fn is not None:
            fn()
        for key, src, dst, link, _ in sends:
            remote(key, src, dst, LINKS[link] if isinstance(link, str) else link)
    for d in started[-N_SEND:]:
        d.wait_send()


def in_order(tasks, groups, show=False):
    per_kb = 1024.0 / 48.5e3
    free, came, when = {}, {}, {}
    left = list(tasks)
    out = []
    t = 1.5

    def members(names):
        return [key for w in names for key in (groups[w][0] if w in groups else (w,))]

    while left:
        best = None
        for i, (name, _, waits, after, sends, cost, prio) in enumerate(left):
            keys = members(waits)
            if any(a not in when for a in after) or any(w not in came for w in keys):
                continue
            ready = max([came[w] for w in keys] + [t])
            if name.startswith("bin"):
                ready = max(ready, 2.6 + 0.36 * int(name[3:]))
            if name[0] == "s" and name[1].isdigit():
                ready = max([ready] + [free.get(v[3], 0.0) - BACKLOG for v in sends])
            rank = (ready > t, ready if ready > t else 0.0, -prio, i)
            if best is None or rank < best[0]:
                best = (rank, i, ready)
        _, i, ready = best
        item = left.pop(i)
        name, _, waits, _, sends, cost, _ = item
        t = ready + cost + 0.02 * len(waits)
        for key, _, _, link, kb in sends:
            t += 0.04
            if not isinstance(link, str):
                came[key] = t + 2.6
                continue
            hops = {"pc": 0}.get(link, 2 if link[1] == "2" else 1)
            lane = link[0] + "+" if hops == 2 else link
            busy = kb * 1024.0 / 500e3 if link == "pc" else kb * per_kb * hops
            start = max(t, free.get(lane, 0.0))
            free[lane] = start + busy
            came[key] = start + busy + (0.9, 1.7, 2.5)[hops]
        when[name] = t
        out.append(item)
        if show:
            print("%7.2f %s" % (t, name))
    return out


BACKLOG = 1.0
N_SEND = 48
N_RECV = 125
N_LOCAL = 16


def exchange(raw, off, gain, sec, cell, tomograms, count, group):
    vmem = pl.BlockSpec(memory_space=pltpu.VMEM)
    any_ = pl.BlockSpec(memory_space=pltpu.HBM)
    return pl.pallas_call(
        comm_kernel,
        in_specs=[any_] * 9,
        out_specs=[vmem] * 5,
        out_shape=[
            pltpu.VMEM((KC, 4, 2, FX, FC, PB), BF16),
            pltpu.VMEM((KC, NR, FX * FC), BF16),
            pltpu.VMEM((NR, SLICE), BF16),
            pltpu.VMEM((NR, SLICE), F32),
            pltpu.VMEM((FX, 8, NF // FX), F32),
        ],
        scratch_shapes=[
            pltpu.VMEM((NBUF, BT, NC, PIXSUB, PB), BF16),
            pltpu.VMEM((3, NC, PIXSUB, PB), BF16),
            pltpu.VMEM((3, NC, PIXSUB, PB), BF16),
            pltpu.VMEM((NC, PIXSUB, PB), jnp.int32),
            pltpu.VMEM((NC, PIXSUB, PB), F32),
            pltpu.VMEM((NC, 8, PB), F32),
            pltpu.VMEM((PB // 128, BT * NC * 8, 128), F32),
            pltpu.VMEM((NF, PB), BF16),
            pltpu.VMEM((NQ, 4, FR, PB), BF16),
            pltpu.VMEM((NR, SLICE), BF16),
            pltpu.VMEM((KC, NR, FX * FC), F32),
            pltpu.VMEM((KC, 2, NR // 2, FC), F32),
            pltpu.VMEM((KC, 2, NR, FC), F32),
            pltpu.VMEM((KC, 2, NR // 2, FC), F32),
            pltpu.VMEM((KC, NR, FC), F32),
            pltpu.VMEM((KC, 1, FC), F32),
            pltpu.VMEM((KC, 8, 2, FC), F32),
            pltpu.VMEM((KC, 4, 2, FC), F32),
            pltpu.VMEM((FX, 8, NF // FX), F32),
            pltpu.SMEM((NC, NT), jnp.int32),
            pltpu.SMEM((NT,), jnp.int32),
            pltpu.VMEM((1, NT), jnp.int32),
            pltpu.VMEM((1, NT), jnp.int32),
            pltpu.SemaphoreType.DMA((N_SEND,)),
            pltpu.SemaphoreType.DMA((N_RECV,)),
            pltpu.SemaphoreType.DMA((N_LOCAL,)),
            pltpu.SemaphoreType.DMA((NBUF,)),
        ],
        compiler_params=pltpu.CompilerParams(
            collective_id=0, has_side_effects=True, vmem_limit_bytes=45 << 20
        ),
        name="exchange",
    )(cell.T, count, raw, off, gain, sec, tomograms, count.reshape(1, NT), group.reshape(1, NT))


def update_kernel(pat_ref, resp_ref, tomo_ref, num_ref, ll_ref, out_ref, llo_ref, inv_s):
    step = pl.program_id(0)

    @pl.when(step == 0)
    def _():
        total = None
        for k in range(KC):
            part = jnp.sum(resp_ref[k].astype(F32), axis=1, keepdims=True)
            total = part if total is None else total + part
        inv_s[...] = 1.0 / (total + SMOOTHING)
        llo_ref[...] = jnp.concatenate([ll_ref[b, 0:1, :] for b in range(FX)], axis=1)

    columns = pl.ds(pl.multiple_of(step * PB, PB), PB)
    total = num_ref[:, columns] + jnp.dot(
        resp_ref[KC - 1], pat_ref[KC - 1, step // 2, step % 2].reshape(FX * FC, PB),
        preferred_element_type=F32,
    )
    out_ref[...] = (total + SMOOTHING * tomo_ref[:, columns].astype(F32)) * inv_s[...]


def update(pat, resp, tomo, num, ll):
    vmem = pl.BlockSpec(memory_space=pltpu.VMEM)
    return pl.pallas_call(
        update_kernel,
        grid=(8,),
        in_specs=[vmem] * 5,
        out_specs=[
            pl.BlockSpec((NR, PB), lambda i: (0, i)),
            pl.BlockSpec((1, NF), lambda i: (0, 0)),
        ],
        out_shape=[
            jax.ShapeDtypeStruct((NR, SLICE), F32),
            jax.ShapeDtypeStruct((1, NF), F32),
        ],
        scratch_shapes=[pltpu.VMEM((NR, 1), F32)],
        compiler_params=pltpu.CompilerParams(vmem_limit_bytes=24 << 20),
        name="update",
    )(pat, resp, tomo, num, ll)


def on_device(
    raw_frames, offset_table, gain_table, gain_section, hit_cell, hit_count, train_group, tomograms
):
    pat, resp, tomo, num, ll = exchange(
        raw_frames, offset_table, gain_table, gain_section, hit_cell, tomograms,
        hit_count, train_group,
    )
    new_tomograms, loglik = update(pat, resp, tomo, num, ll)
    return new_tomograms, loglik.reshape(NF)


def solution(mesh):
    placed = (
        P("frames", None, None, "orient"),
        P(None, None, None, "orient"),
        P(None, None, None, "orient"),
        P(None, None, "orient"),
        P("frames", None),
        P("frames"),
        P("frames"),
        P("orient", None),
    )
    return jax.shard_map(
        on_device,
        mesh=mesh,
        in_specs=placed,
        out_specs=(P("orient", "frames"), P("frames")),
        check_vma=False,
    )
```

```python
import functools
import math

import jax
import jax.numpy as jnp
from jax import lax
from jax.experimental import pallas as pl
from jax.experimental.pallas import tpu as pltpu
from jax.sharding import PartitionSpec as P

NPIX = 16384
PIXSUB = 64
SMOOTHING = 0.1
SCALE = 1.2 / math.sqrt(NPIX * PIXSUB)

MESH = pl.DeviceIdType.MESH
F32 = jnp.float32
BF16 = jnp.bfloat16

FX = 4
NT = 64
NC = 4
NF = NT * NC
PB = 512
NR = 256
SLICE = NPIX // FX
KC = 2
QC = 2
NQ = KC * QC
FR = NF // 4 // NQ
FC = NF // KC


BT = 4
NSTEP = NT // BT
NBUF = 6
PARTS = (2, 1, 3, 0)


def comm_kernel(
    cell_in, count_in, raw_ref, off_ref, gain_ref, sec_ref, tomo_ref, count_row, group_row,
    pat, resp, tomo, num, llrecv,
    rawb, offb, gainb, secb, gain_s, og_s, acc_s, bin_ref,
    tz, logt, sall, far, near, own, wexp, high_s, staty, statz, llsend,
    cell_ref, count_s, count_ref, group_ref,
    ssem, rsem, lsem, rawsem,
):
    x = lax.axis_index("frames")
    o = lax.axis_index("orient")
    z = o // 8
    y = (o // 2) % 4
    c = o % 2

    def dev(dx=0, dz=0, dy=0, flip=False):
        cc = 1 - c if flip else c
        return ((x + dx) % 4, ((z + dz) % 4) * 8 + ((y + dy) % 4) * 2 + cc)

    def wrap(v, d):
        return (v + d) % 4

    started = []
    used = [0, 0]

    group_of, groups, sem_of = {}, {}, {}

    def group(name, keys, ref):
        groups[name] = (tuple(keys), ref)
        for key in keys:
            group_of[key] = name

    def remote(key, src, dst, device):
        n = used[0]
        used[0] += 1
        if n >= N_SEND:
            started[n - N_SEND].wait_send()
        sem = sem_of.setdefault(group_of.get(key, key), len(sem_of))
        d = pltpu.make_async_remote_copy(
            src_ref=src, dst_ref=dst, send_sem=ssem.at[n % N_SEND], recv_sem=rsem.at[sem],
            device_id=device, device_id_type=MESH,
        )
        d.start()
        started.append(d)
        arrivals[key] = d

    def await_arrival(name):
        if name in groups:
            keys, ref = groups[name]
            assert all(key in arrivals for key in keys)
            pltpu.make_async_copy(ref, ref, rsem.at[sem_of[name]]).wait()
        else:
            arrivals[name].wait_recv()

    def local(src, dst):
        n = used[1]
        used[1] += 1
        d = pltpu.make_async_copy(src, dst, lsem.at[n])
        d.start()
        return d

    barrier = pltpu.get_barrier_semaphore()
    peers = [dev(dx=d) for d in (1, 2, 3)] + [dev(dz=d) for d in (1, 2, 3)]
    peers += [dev(dy=d, flip=f) for d in range(4) for f in (False, True) if d or f]
    for p in peers:
        pl.semaphore_signal(barrier, inc=1, device_id=p, device_id_type=MESH)

    small_copies = [
        local(cell_in, cell_ref), local(count_in, count_s),
        local(count_row, count_ref), local(group_row, group_ref),
    ]
    table_copies = [local(sec_ref, secb), local(gain_ref, gainb), local(off_ref, offb)]
    steps = [(q, d, h) for q in range(NQ) for d in PARTS for h in range(NSTEP // NQ // 4)]

    def first_train(n):
        q, d, h = steps[n]
        return wrap(z, d) * (NT // 4) + q * (NT // 4 // NQ) + h * BT

    def fetch(n):
        first = first_train(n)
        return pltpu.make_async_copy(
            raw_ref.at[pl.ds(first, BT)], rawb.at[n % NBUF], rawsem.at[n % NBUF]
        )

    for n in range(NBUF):
        fetch(n).start()

    for m in table_copies + small_copies:
        m.wait()

    def cell_tables(c, carry):
        part = None
        for r in range(PIXSUB // 8):
            rows = slice(r * 8, r * 8 + 8)
            sec = secb[c, rows]

            def chosen(table):
                return jnp.where(
                    sec == 0,
                    table[0, c, rows].astype(F32),
                    jnp.where(sec == 1, table[1, c, rows].astype(F32), table[2, c, rows].astype(F32)),
                )

            g = chosen(gainb)
            gain_s[c, rows] = g
            term = chosen(offb) * g
            part = term if part is None else part + term
        og_s[c] = part
        return carry

    lax.fori_loop(0, NC, cell_tables, 0)

    def bin_step(n):
        first = first_train(n)
        fetch(n).wait()
        if n == NSTEP - NBUF:
            columns = pl.ds(pl.multiple_of(x * SLICE, SLICE), SLICE)
            kept["tomo"] = local(tomo_ref.at[:, columns], tomo)
        buf = n % NBUF

        def train(i, carry):
            count = count_s[first + i]
            for slot in range(NC):
                c = cell_ref[slot, first + i]
                part = None
                for r in range(PIXSUB // 16):
                    v = rawb[buf, i, slot, r * 16:r * 16 + 16].astype(F32)
                    v = v * gain_s[c, r * 16:r * 16 + 16]
                    v = v[0:8] + v[8:16]
                    part = v if part is None else part + v
                part = jnp.where(slot < count, part - og_s[c], 0.0)
                for l in range(PB // 128):
                    row = pl.multiple_of((i * NC + slot) * 8, 8)
                    acc_s[l, pl.ds(row, 8), :] = part[:, l * 128:l * 128 + 128]
            return carry

        lax.fori_loop(0, BT, train, 0)
        row = pl.multiple_of(first * NC, BT * NC)
        for l in range(PB // 128):
            total = None
            for i in range(8):
                part = acc_s[l, pl.ds(i, BT * NC, stride=8), :]
                total = part if total is None else total + part
            bin_ref[pl.ds(row, BT * NC), l * 128:l * 128 + 128] = total.astype(BF16)
        if n + NBUF < NSTEP:
            fetch(n + NBUF).start()

    tasks = []
    arrivals = {}

    def task(name, fn=None, waits=(), after=(), sends=(), cost=0.0, prio=0):
        tasks.append((name, fn, tuple(waits), tuple(after), tuple(sends), cost, prio))

    def piece(q, yy, zz, b0, nb):
        row = pl.multiple_of((q % QC) * 4 * FR + zz * FR, FR)
        return pat.at[q // QC, yy, c, pl.ds(b0, nb), pl.ds(row, FR), :]

    def rows_of(q, zz):
        return bin_ref.at[pl.ds(pl.multiple_of(zz * (NF // 4) + q * FR, FR), FR), :]

    LINKS = {
        "x+": dev(dx=1), "x-": dev(dx=3), "x2": dev(dx=2), "z+": dev(dz=1), "z-": dev(dz=3),
        "z2": dev(dz=2), "y+": dev(dy=1), "y-": dev(dy=3), "pc": dev(flip=True),
    }

    def snd(key, src, dst, link, kb):
        return (key, src, dst, link, kb)

    def same(key, ref, link, kb):
        return (key, ref, ref, link, kb)

    per = NSTEP // NQ // 4
    kept = {}

    def wait_barrier():
        pl.semaphore_wait(barrier, len(peers))

    task("bar", wait_barrier, after=["bin%d" % (per - 1)], cost=0.1)
    PK = FR * PB * 2 / 1024.0
    for n in range(NSTEP):
        task("bin%d" % n, functools.partial(bin_step, n), after=["bin%d" % (n - 1)] if n else [], cost=0.42)

    def keep_local(name, src, dst):
        kept[name] = local(src, dst)

    for q in range(NQ):
        for i, d in enumerate(PARTS):
            last = min((q * 4 + i + 1) * per, NSTEP - 1)
            after = ["bin%d" % last, "bar"]
            src, dst = rows_of(q, wrap(z, d)), tz.at[q, z]
            name = "z%d.%d" % (q, d)
            if d == 0:
                task(name, functools.partial(keep_local, name, src, dst), after=after, cost=0.03, prio=3)
            else:
                link = ("", "z+", "z2", "z-")[d]
                task(name, after=after, sends=[snd(name, src, dst, link, PK)], prio=3)

        here = pat.at[
            q // QC, y, c, x, pl.ds(pl.multiple_of((q % QC) * 4 * FR + z * FR, FR), FR), :
        ]

        def start_own(q=q, here=here):
            kept["z%d.0" % q].wait()
            kept["x%d" % q] = local(tz.at[q, x], here)

        group("zg%d" % q, ["z%d.%d" % (q, d) for d in (2, 1, 3)], tz.at[q, 0:3])
        group("xg%d" % q, ["x%d.%d" % (q, d) for d in (2, 1, 3)], tz.at[q, 0:3])
        task(
            "x%d" % q, start_own, waits=["zg%d" % q], after=["z%d.0" % q],
            sends=[
                snd("x%d.%d" % (q, d), tz.at[q, wrap(x, d)], here, ("", "x+", "x2", "x-")[d], PK)
                for d in (2, 1, 3)
            ], prio=3, cost=0.03,
        )

    A, B = 0, 2
    offs = (0, 3, 1, 2)

    def cast(q):
        def nm(t, *ids):
            return t + str(q) + "".join("." + str(i) for i in ids)

        ra, rb = piece(q, y, z, A, 2), piece(q, y, z, B, 2)
        task(
            nm("s"), lambda: kept["x%d" % q].wait(), waits=["xg%d" % q],
            after=["x%d" % q],
            sends=[
                same(nm("a1", 0), ra, "y+", 2 * PK), same(nm("a1", 1), ra, "y-", 2 * PK),
                same(nm("b1", 0), rb, "z+", 2 * PK), same(nm("b1", 1), rb, "z-", 2 * PK),
                same(nm("a3", 0, 0), ra, "z+", 2 * PK), same(nm("a3", 0, 1), ra, "z-", 2 * PK),
                same(nm("b3", 0, 0), rb, "y+", 2 * PK), same(nm("b3", 0, 1), rb, "y-", 2 * PK),
                same(nm("p", 0), piece(q, y, z, A, 4), "pc", 4 * PK),
            ], prio=2,
        )
        for h, (fy, fz) in enumerate((("y+", "z+"), ("y-", "z-"))):
            d = offs[h + 1]
            r, p = piece(q, wrap(y, d), z, A, 2), piece(q, wrap(y, d), z, A + h, 1)
            task(
                nm("ha", h), waits=[nm("a1", h)],
                sends=[
                    same(nm("a2", h), p, fy, PK),
                    same(nm("a3", h + 1, 0), r, "z+", 2 * PK), same(nm("a3", h + 1, 1), r, "z-", 2 * PK),
                    same(nm("p", 1 + h), r, "pc", 2 * PK),
                ], prio=2,
            )
            r, p = piece(q, y, wrap(z, d), B, 2), piece(q, y, wrap(z, d), B + h, 1)
            task(
                nm("hb", h), waits=[nm("b1", h)],
                sends=[
                    same(nm("b2", h), p, fz, PK),
                    same(nm("b3", h + 1, 0), r, "y+", 2 * PK), same(nm("b3", h + 1, 1), r, "y-", 2 * PK),
                    same(nm("p", 3 + h), r, "pc", 2 * PK),
                ], prio=2,
            )
        r = piece(q, wrap(y, 2), z, A, 2)
        group(nm("a2"), [nm("a2", 0), nm("a2", 1)], r)
        task(
            nm("ia"), waits=[nm("a2")],
            sends=[
                same(nm("a3", 3, 0), r, "z+", 2 * PK), same(nm("a3", 3, 1), r, "z-", 2 * PK),
                same(nm("p", 5), r, "pc", 2 * PK),
            ], prio=2,
        )
        r = piece(q, y, wrap(z, 2), B, 2)
        group(nm("b2"), [nm("b2", 0), nm("b2", 1)], r)
        task(
            nm("ib"), waits=[nm("b2")],
            sends=[
                same(nm("b3", 3, 0), r, "y+", 2 * PK), same(nm("b3", 3, 1), r, "y-", 2 * PK),
                same(nm("p", 6), r, "pc", 2 * PK),
            ], prio=2,
        )

        def column(zz):
            row = pl.multiple_of((q % QC) * 4 * FR + zz * FR, FR)
            return pat.at[q // QC, :, c, pl.ds(A, 2), pl.ds(row, FR), :]

        def line(yy):
            return pat.at[q // QC, yy, c, pl.ds(B, 2), pl.ds((q % QC) * 4 * FR, 4 * FR), :]

        for h, (fy, fz) in enumerate((("y+", "z+"), ("y-", "z-"))):
            e = offs[h + 1]
            for i in range(4):
                d = offs[i]
                task(
                    nm("ja", i, h), waits=[nm("a3", i, h)],
                    sends=[same(nm("a4", i, h), piece(q, wrap(y, d), wrap(z, e), A + h, 1), fz, PK)],
                    prio=2,
                )
                task(
                    nm("jb", i, h), waits=[nm("b3", i, h)],
                    sends=[same(nm("b4", i, h), piece(q, wrap(y, e), wrap(z, d), B + h, 1), fy, PK)],
                    prio=2,
                )
            task(
                nm("ka", h), after=[nm("ja", i, h) for i in range(4)],
                sends=[same(nm("p", 7 + h), column(wrap(z, e)), "pc", 8 * PK)], prio=1,
            )
            task(
                nm("kb", h), after=[nm("jb", i, h) for i in range(4)],
                sends=[same(nm("p", 9 + h), line(wrap(y, e)), "pc", 8 * PK)], prio=1,
            )
        group(nm("a4"), [nm("a4", i, h) for i in range(4) for h in range(2)], column(wrap(z, 2)))
        group(nm("b4"), [nm("b4", i, h) for i in range(4) for h in range(2)], line(wrap(y, 2)))
        rows = pl.ds((q % QC) * 4 * FR, 4 * FR)
        group(nm("p"), [nm("p", i) for i in range(13)], pat.at[q // QC, :, 1 - c, :, rows, :])
        task(
            nm("la"), waits=[nm("a4")],
            sends=[same(nm("p", 11), column(wrap(z, 2)), "pc", 8 * PK)], prio=2,
        )
        task(
            nm("lb"), waits=[nm("b4")],
            sends=[same(nm("p", 12), line(wrap(y, 2)), "pc", 8 * PK)], prio=2,
        )
        task(nm("done"), waits=[nm("p")], after=[nm("la"), nm("lb")], prio=5)

    for q in range(NQ):
        cast(q)

    def log_block(i):
        if i == 0:
            kept["tomo"].wait()
        cols = slice(i * PB, (i + 1) * PB)
        logt[:, cols] = jnp.log(tomo[:, cols].astype(F32)).astype(BF16)

    for i in range(8):
        task(
            "log%d" % i, functools.partial(log_block, i),
            after=["log%d" % (i - 1)] if i else ["bin%d" % (NSTEP - 1)], cost=0.35,
        )

    HR = NR // 2

    def lanes(d):
        return pl.ds(pl.multiple_of(wrap(x, d) * FC, FC), FC)

    infos = {}

    def slot_info(k):
        lane = lax.broadcasted_iota(jnp.int32, (NT, FC), 1)
        frame = (lane % (4 * FR)) // FR * (NF // 4) + (k * QC + lane // (4 * FR)) * FR + lane % FR
        train_of = frame // NC
        row = lax.broadcasted_iota(jnp.int32, (NT, FC), 0)
        pick = (row == train_of).astype(F32)
        ahead = (row < train_of).astype(F32)
        count = count_ref[...].astype(F32)
        group = group_ref[...].astype(F32)
        by_group = [jnp.where(group == float(g), count, 0.0) for g in range(FX)]
        weights = jnp.concatenate(by_group + [count, group, count, group], axis=0)

        def mul(m):
            return lax.dot_general(
                weights, m, (((1,), (0,)), ((), ())),
                preferred_element_type=F32, precision=lax.Precision.HIGHEST,
            )

        here, before = mul(pick), mul(ahead)
        own_group = here[5:6]
        slot = (frame[0:1] % NC).astype(F32)
        live = (slot < here[4:5]).astype(F32)
        place = slot
        for g in range(FX):
            place = place + jnp.where(own_group == float(g), before[g:g + 1], 0.0)
        infos[k] = (live, jnp.where(live > 0.0, place, -1.0), own_group)

    loglik = {}

    def scores_chain(k):
        def nm(t, *ids):
            return t + "k" + str(k) + "".join("." + str(i) for i in ids)

        task(nm("info"), functools.partial(slot_info, k), after=["bin%d" % (NSTEP - 1)], cost=0.5, prio=-1)

        def dots():
            total = None
            for yy in range(4):
                for cc in range(2):
                    blk = yy * 2 + cc
                    part = lax.dot_general(
                        logt[:, blk * PB:(blk + 1) * PB],
                        pat[k, yy, cc].reshape(FX * FC, PB),
                        (((1,), (1,)), ((), ())),
                        preferred_element_type=F32,
                    )
                    total = part if total is None else total + part
            sall[k] = total

        SK = HR * FC * 4 / 1024.0
        task(
            nm("dots"), dots, after=["done%d" % (k * QC + i) for i in range(QC)] + ["log7"], cost=0.8, prio=1,
            sends=[
                snd(nm("far", 0), sall.at[k, 0:HR, lanes(2)], far.at[k, 0], "x+", SK),
                snd(nm("far", 1), sall.at[k, HR:NR, lanes(2)], far.at[k, 1], "x-", SK),
                snd(nm("near", 0), sall.at[k, HR:NR, lanes(1)], near.at[k, 0, HR:NR], "x+", SK),
                snd(nm("near", 1), sall.at[k, 0:HR, lanes(3)], near.at[k, 1, 0:HR], "x-", SK),
            ],
        )

        def add(h):
            rows, d = ((slice(0, HR), 1), (slice(HR, NR), 3))[h]
            own[k, h] = sall[k, rows, lanes(d)] + far[k, h]

        task(
            nm("add", 0), functools.partial(add, 0), waits=[nm("far", 0)], cost=0.05, prio=2,
            sends=[snd(nm("near", 2), own.at[k, 0], near.at[k, 0, 0:HR], "x+", SK)],
        )
        task(
            nm("add", 1), functools.partial(add, 1), waits=[nm("far", 1)], cost=0.05, prio=2,
            sends=[snd(nm("near", 3), own.at[k, 1], near.at[k, 1, HR:NR], "x-", SK)],
        )

        def stats1():
            scores = (sall[k, :, lanes(0)] + near[k, 0] + near[k, 1]) * SCALE
            high = jnp.max(scores, axis=0, keepdims=True)
            weights = jnp.exp(scores - high)
            wexp[k] = weights
            mine = staty.at[k, y * 2 + c]
            mine[0:1, :] = high
            mine[1:2, :] = jnp.sum(weights, axis=0, keepdims=True)
            high_s[k] = high

        group(nm("near"), [nm("near", i) for i in range(4)], near.at[k])
        group(nm("sy"), [nm("sy", d, f) for d in range(4) for f in range(2) if d or f], staty.at[k, 0:7])
        group(nm("sz"), [nm("sz", d) for d in (1, 2, 3)], statz.at[k, 0:3])
        group(nm("r2"), [nm("r2", 0), nm("r2", 1)], resp.at[k, :, lanes(2)])
        mine = staty.at[k, y * 2 + c]
        task(
            nm("st1"), stats1, waits=[nm("near")], cost=0.3, prio=2,
            sends=[
                snd(nm("sy", d, f), mine, mine, dev(dy=d, flip=bool(f)), 1.0)
                for d in range(4) for f in range(2) if d or f
            ],
        )

        def merge(ref):
            highs, sums = ref[k, :, 0, :], ref[k, :, 1, :]
            high = jnp.max(highs, axis=0, keepdims=True)
            return high, jnp.sum(sums * jnp.exp(highs - high), axis=0, keepdims=True)

        def stats2():
            high, total = merge(staty)
            mine = statz.at[k, z]
            mine[0:1, :] = high
            mine[1:2, :] = total

        minez = statz.at[k, z]
        task(
            nm("st2"), stats2, cost=0.1, prio=2,
            waits=[nm("sy")],
            sends=[snd(nm("sz", d), minez, minez, dev(dz=d), 1.0) for d in (2, 1, 3)],
        )

        def stats3():
            live = infos[k][0]
            highest, partition = merge(statz)
            factor = jnp.exp(high_s[k] - highest) / partition * live
            resp[k, :, lanes(0)] = (wexp[k] * factor).astype(BF16)
            loglik[k] = (highest + jnp.log(partition)) * live

        RK = NR * FC * 2 / 1024.0
        r = resp.at[k, :, lanes(0)]
        task(
            nm("st3"), stats3, waits=[nm("sz")], after=[nm("info")], cost=0.3, prio=2,
            sends=[same(nm("r1", 0), r, "x+", RK), same(nm("r1", 1), r, "x-", RK)],
        )
        task(
            nm("g", 0), waits=[nm("r1", 0)], prio=2,
            sends=[same(nm("r2", 0), resp.at[k, 0:HR, lanes(3)], "x+", RK / 2)],
        )
        task(
            nm("g", 1), waits=[nm("r1", 1)], prio=2,
            sends=[same(nm("r2", 1), resp.at[k, HR:NR, lanes(1)], "x-", RK / 2)],
        )

    for k in range(KC):
        scores_chain(k)

    def place_loglik():
        for g in range(FX):
            total = None
            for k in range(KC):
                _, place, own_group = infos[k]
                slot = lax.broadcasted_iota(jnp.int32, (NF // FX, FC), 0).astype(F32)
                mask = ((slot == place) & (own_group == float(g))).astype(F32)
                part = lax.dot_general(
                    jnp.broadcast_to(loglik[k], (8, FC)), mask, (((1,), (1,)), ((), ())),
                    preferred_element_type=F32, precision=lax.Precision.HIGHEST,
                )
                total = part if total is None else total + part
            llsend[g] = total
        llrecv[x] = llsend[x]

    task(
        "ll", place_loglik, after=["st3k%d" % k for k in range(KC)], cost=0.4, prio=1,
        sends=[snd("ll.%d" % d, llsend.at[wrap(x, d)], llrecv.at[x], dev(dx=d), 2.0) for d in (2, 1, 3)],
    )
    group("llg", ["ll.%d" % d for d in (1, 2, 3)], llrecv.at[0:3])

    def part_of_numerator(i):
        total = None
        for k in range(KC - 1):
            part = jnp.dot(
                resp[k], pat[k, i // 2, i % 2].reshape(FX * FC, PB), preferred_element_type=F32
            )
            total = part if total is None else total + part
        num[:, i * PB:(i + 1) * PB] = total

    for i in range(8):
        before = ["num%d" % (i - 1)] if i else ["gk%d.%d" % (KC - 2, h) for h in range(2)]
        waits = [] if i else ["r2k%d" % k for k in range(KC - 1)]
        task("num%d" % i, functools.partial(part_of_numerator, i), waits=waits, after=before, cost=0.35)
    task(
        "end", waits=["llg", "r2k%d" % (KC - 1)],
        after=["gk%d.%d" % (KC - 1, h) for h in range(2)] + ["num7"],
    )

    for name, fn, waits, _, sends, _, _ in in_order(tasks, groups):
        for w in waits:
            await_arrival(w)
        if fn is not None:
            fn()
        for key, src, dst, link, _ in sends:
            remote(key, src, dst, LINKS[link] if isinstance(link, str) else link)
    for d in started[-N_SEND:]:
        d.wait_send()


def in_order(tasks, groups, show=False):
    per_kb = 1024.0 / 60.0e3
    free, came, when = {}, {}, {}
    left = list(tasks)
    out = []
    t = 1.5

    def members(names):
        return [key for w in names for key in (groups[w][0] if w in groups else (w,))]

    while left:
        best = None
        for i, (name, _, waits, after, sends, cost, prio) in enumerate(left):
            keys = members(waits)
            if any(a not in when for a in after) or any(w not in came for w in keys):
                continue
            ready = max([came[w] for w in keys] + [t])
            if name.startswith("bin"):
                ready = max(ready, 2.6 + 0.36 * int(name[3:]))
            if name[0] == "s" and name[1].isdigit():
                ready = max([ready] + [free.get(v[3], 0.0) - BACKLOG for v in sends])
            rank = (ready > t, ready if ready > t else 0.0, -prio, i)
            if best is None or rank < best[0]:
                best = (rank, i, ready)
        _, i, ready = best
        item = left.pop(i)
        name, _, waits, _, sends, cost, _ = item
        t = ready + cost + 0.02 * len(waits)
        for key, _, _, link, kb in sends:
            t += 0.012
            if not isinstance(link, str):
                came[key] = t + 2.6
                continue
            hops = {"pc": 0}.get(link, 2 if link[1] == "2" else 1)
            lane = link[0] + "+" if hops == 2 else link
            busy = kb * 1024.0 / 500e3 if link == "pc" else kb * per_kb * hops
            start = max(t, free.get(lane, 0.0))
            free[lane] = start + busy
            came[key] = start + busy + (0.9, 1.7, 2.5)[hops]
        when[name] = t
        out.append(item)
        if show:
            print("%7.2f %s" % (t, name))
    return out


BACKLOG = 8.0
N_SEND = 48
N_RECV = 125
N_LOCAL = 16


def exchange(raw, off, gain, sec, cell, tomograms, count, group):
    vmem = pl.BlockSpec(memory_space=pltpu.VMEM)
    any_ = pl.BlockSpec(memory_space=pltpu.HBM)
    return pl.pallas_call(
        comm_kernel,
        in_specs=[any_] * 9,
        out_specs=[vmem] * 5,
        out_shape=[
            pltpu.VMEM((KC, 4, 2, FX, FC, PB), BF16),
            pltpu.VMEM((KC, NR, FX * FC), BF16),
            pltpu.VMEM((NR, SLICE), BF16),
            pltpu.VMEM((NR, SLICE), F32),
            pltpu.VMEM((FX, 8, NF // FX), F32),
        ],
        scratch_shapes=[
            pltpu.VMEM((NBUF, BT, NC, PIXSUB, PB), BF16),
            pltpu.VMEM((3, NC, PIXSUB, PB), BF16),
            pltpu.VMEM((3, NC, PIXSUB, PB), BF16),
            pltpu.VMEM((NC, PIXSUB, PB), jnp.int32),
            pltpu.VMEM((NC, PIXSUB, PB), F32),
            pltpu.VMEM((NC, 8, PB), F32),
            pltpu.VMEM((PB // 128, BT * NC * 8, 128), F32),
            pltpu.VMEM((NF, PB), BF16),
            pltpu.VMEM((NQ, 4, FR, PB), BF16),
            pltpu.VMEM((NR, SLICE), BF16),
            pltpu.VMEM((KC, NR, FX * FC), F32),
            pltpu.VMEM((KC, 2, NR // 2, FC), F32),
            pltpu.VMEM((KC, 2, NR, FC), F32),
            pltpu.VMEM((KC, 2, NR // 2, FC), F32),
            pltpu.VMEM((KC, NR, FC), F32),
            pltpu.VMEM((KC, 1, FC), F32),
            pltpu.VMEM((KC, 8, 2, FC), F32),
            pltpu.VMEM((KC, 4, 2, FC), F32),
            pltpu.VMEM((FX, 8, NF // FX), F32),
            pltpu.SMEM((NC, NT), jnp.int32),
            pltpu.SMEM((NT,), jnp.int32),
            pltpu.VMEM((1, NT), jnp.int32),
            pltpu.VMEM((1, NT), jnp.int32),
            pltpu.SemaphoreType.DMA((N_SEND,)),
            pltpu.SemaphoreType.DMA((N_RECV,)),
            pltpu.SemaphoreType.DMA((N_LOCAL,)),
            pltpu.SemaphoreType.DMA((NBUF,)),
        ],
        compiler_params=pltpu.CompilerParams(
            collective_id=0, has_side_effects=True, vmem_limit_bytes=45 << 20
        ),
        name="exchange",
    )(cell.T, count, raw, off, gain, sec, tomograms, count.reshape(1, NT), group.reshape(1, NT))


WIDE = 4


def update_kernel(pat_ref, resp_ref, tomo_ref, num_ref, ll_ref, out_ref, llo_ref, inv_s):
    step = pl.program_id(0)

    @pl.when(step == 0)
    def _():
        total = None
        for k in range(KC):
            part = jnp.sum(resp_ref[k].astype(F32), axis=1, keepdims=True)
            total = part if total is None else total + part
        inv_s[...] = 1.0 / (total + SMOOTHING)
        llo_ref[...] = jnp.concatenate([ll_ref[b, 0:1, :] for b in range(FX)], axis=1)

    for h in range(WIDE):
        block = step * WIDE + h
        columns = pl.ds(pl.multiple_of(block * PB, PB), PB)
        total = num_ref[:, columns] + jnp.dot(
            resp_ref[KC - 1], pat_ref[KC - 1, block // 2, block % 2].reshape(FX * FC, PB),
            preferred_element_type=F32,
        )
        total = total + SMOOTHING * tomo_ref[:, columns].astype(F32)
        out_ref[:, h * PB:(h + 1) * PB] = total * inv_s[...]


def update(pat, resp, tomo, num, ll):
    vmem = pl.BlockSpec(memory_space=pltpu.VMEM)
    return pl.pallas_call(
        update_kernel,
        grid=(8 // WIDE,),
        in_specs=[vmem] * 5,
        out_specs=[
            pl.BlockSpec((NR, WIDE * PB), lambda i: (0, i)),
            pl.BlockSpec((1, NF), lambda i: (0, 0)),
        ],
        out_shape=[
            jax.ShapeDtypeStruct((NR, SLICE), F32),
            jax.ShapeDtypeStruct((1, NF), F32),
        ],
        scratch_shapes=[pltpu.VMEM((NR, 1), F32)],
        compiler_params=pltpu.CompilerParams(vmem_limit_bytes=24 << 20),
        name="update",
    )(pat, resp, tomo, num, ll)


def on_device(
    raw_frames, offset_table, gain_table, gain_section, hit_cell, hit_count, train_group, tomograms
):
    pat, resp, tomo, num, ll = exchange(
        raw_frames, offset_table, gain_table, gain_section, hit_cell, tomograms,
        hit_count, train_group,
    )
    new_tomograms, loglik = update(pat, resp, tomo, num, ll)
    return new_tomograms, loglik.reshape(NF)


def solution(mesh):
    placed = (
        P("frames", None, None, "orient"),
        P(None, None, None, "orient"),
        P(None, None, None, "orient"),
        P(None, None, "orient"),
        P("frames", None),
        P("frames"),
        P("frames"),
        P("orient", None),
    )
    return jax.shard_map(
        on_device,
        mesh=mesh,
        in_specs=placed,
        out_specs=(P("orient", "frames"), P("frames")),
        check_vma=False,
    )
```

```python
import functools
import math

import jax
import jax.numpy as jnp
from jax import lax
from jax.experimental import pallas as pl
from jax.experimental.pallas import tpu as pltpu
from jax.sharding import PartitionSpec as P

NPIX = 16384
PIXSUB = 64
SMOOTHING = 0.1
SCALE = 1.2 / math.sqrt(NPIX * PIXSUB)

MESH = pl.DeviceIdType.MESH
F32 = jnp.float32
BF16 = jnp.bfloat16

FX = 4
NT = 64
NC = 4
NF = NT * NC
PB = 512
NR = 256
SLICE = NPIX // FX
KC = 2
QC = 2
NQ = KC * QC
FR = NF // 4 // NQ
FC = NF // KC


BT = 4
NSTEP = NT // BT
NBUF = 4
PARTS = (2, 1, 3, 0)


def comm_kernel(
    cell_in, count_in, raw_ref, off_ref, gain_ref, sec_ref, tomo_ref, count_row, group_row,
    pat, resp, tomo, num, llrecv,
    rawb, offb, gainb, secb, gain_s, og_s, acc_s, bin_ref,
    tz, logt, sall, far, near, own, wexp, high_s, staty, statz, llsend,
    cell_ref, count_s, count_ref, group_ref,
    ssem, rsem, lsem, rawsem,
):
    x = lax.axis_index("frames")
    o = lax.axis_index("orient")
    z = o // 8
    y = (o // 2) % 4
    c = o % 2

    def dev(dx=0, dz=0, dy=0, flip=False):
        cc = 1 - c if flip else c
        return ((x + dx) % 4, ((z + dz) % 4) * 8 + ((y + dy) % 4) * 2 + cc)

    def wrap(v, d):
        return (v + d) % 4

    started = []
    used = [0, 0]

    group_of, groups, sem_of = {}, {}, {}

    def group(name, keys, ref):
        groups[name] = (tuple(keys), ref)
        for key in keys:
            group_of[key] = name

    def remote(key, src, dst, device):
        n = used[0]
        used[0] += 1
        if n >= N_SEND:
            started[n - N_SEND].wait_send()
        sem = sem_of.setdefault(group_of.get(key, key), len(sem_of))
        d = pltpu.make_async_remote_copy(
            src_ref=src, dst_ref=dst, send_sem=ssem.at[n % N_SEND], recv_sem=rsem.at[sem],
            device_id=device, device_id_type=MESH,
        )
        d.start()
        started.append(d)
        arrivals[key] = d

    def await_arrival(name):
        if name in groups:
            keys, ref = groups[name]
            assert all(key in arrivals for key in keys)
            pltpu.make_async_copy(ref, ref, rsem.at[sem_of[name]]).wait()
        else:
            arrivals[name].wait_recv()

    def local(src, dst):
        n = used[1]
        used[1] += 1
        d = pltpu.make_async_copy(src, dst, lsem.at[n])
        d.start()
        return d

    barrier = pltpu.get_barrier_semaphore()
    peers = [dev(dx=d) for d in (1, 2, 3)] + [dev(dz=d) for d in (1, 2, 3)]
    peers += [dev(dy=d, flip=f) for d in range(4) for f in (False, True) if d or f]
    for p in peers:
        pl.semaphore_signal(barrier, inc=1, device_id=p, device_id_type=MESH)

    small_copies = [
        local(cell_in, cell_ref), local(count_in, count_s),
        local(count_row, count_ref), local(group_row, group_ref),
    ]
    table_copies = [local(sec_ref, secb), local(gain_ref, gainb), local(off_ref, offb)]
    steps = [(q, d, h) for q in range(NQ) for d in PARTS for h in range(NSTEP // NQ // 4)]

    def first_train(n):
        q, d, h = steps[n]
        return wrap(z, d) * (NT // 4) + q * (NT // 4 // NQ) + h * BT

    def fetch(n):
        first = first_train(n)
        return pltpu.make_async_copy(
            raw_ref.at[pl.ds(first, BT)], rawb.at[n % NBUF], rawsem.at[n % NBUF]
        )

    for n in range(NBUF):
        fetch(n).start()

    for m in table_copies + small_copies:
        m.wait()

    def cell_tables(c, carry):
        part = None
        for r in range(PIXSUB // 8):
            rows = slice(r * 8, r * 8 + 8)
            sec = secb[c, rows]

            def chosen(table):
                return jnp.where(
                    sec == 0,
                    table[0, c, rows].astype(F32),
                    jnp.where(sec == 1, table[1, c, rows].astype(F32), table[2, c, rows].astype(F32)),
                )

            g = chosen(gainb)
            gain_s[c, rows] = g
            term = chosen(offb) * g
            part = term if part is None else part + term
        og_s[c] = part
        return carry

    lax.fori_loop(0, NC, cell_tables, 0)

    def bin_step(n):
        first = first_train(n)
        fetch(n).wait()
        if n == NSTEP - NBUF:
            columns = pl.ds(pl.multiple_of(x * SLICE, SLICE), SLICE)
            kept["tomo"] = local(tomo_ref.at[:, columns], tomo)
        buf = n % NBUF

        def train(i, carry):
            count = count_s[first + i]
            for slot in range(NC):
                c = cell_ref[slot, first + i]
                part = None
                for r in range(PIXSUB // 16):
                    v = rawb[buf, i, slot, r * 16:r * 16 + 16].astype(F32)
                    v = v * gain_s[c, r * 16:r * 16 + 16]
                    v = v[0:8] + v[8:16]
                    part = v if part is None else part + v
                part = jnp.where(slot < count, part - og_s[c], 0.0)
                for l in range(PB // 128):
                    row = pl.multiple_of((i * NC + slot) * 8, 8)
                    acc_s[l, pl.ds(row, 8), :] = part[:, l * 128:l * 128 + 128]
            return carry

        lax.fori_loop(0, BT, train, 0)
        row = pl.multiple_of(first * NC, BT * NC)
        for l in range(PB // 128):
            total = None
            for i in range(8):
                part = acc_s[l, pl.ds(i, BT * NC, stride=8), :]
                total = part if total is None else total + part
            bin_ref[pl.ds(row, BT * NC), l * 128:l * 128 + 128] = total.astype(BF16)
        if n + NBUF < NSTEP:
            fetch(n + NBUF).start()

    tasks = []
    arrivals = {}

    def task(name, fn=None, waits=(), after=(), sends=(), cost=0.0, prio=0):
        tasks.append((name, fn, tuple(waits), tuple(after), tuple(sends), cost, prio))

    def piece(q, yy, zz, b0, nb):
        row = pl.multiple_of((q % QC) * 4 * FR + zz * FR, FR)
        return pat.at[q // QC, yy, c, pl.ds(b0, nb), pl.ds(row, FR), :]

    def rows_of(q, zz):
        return bin_ref.at[pl.ds(pl.multiple_of(zz * (NF // 4) + q * FR, FR), FR), :]

    LINKS = {
        "x+": dev(dx=1), "x-": dev(dx=3), "x2": dev(dx=2), "z+": dev(dz=1), "z-": dev(dz=3),
        "z2": dev(dz=2), "y+": dev(dy=1), "y-": dev(dy=3), "pc": dev(flip=True),
    }

    def snd(key, src, dst, link, kb):
        return (key, src, dst, link, kb)

    def same(key, ref, link, kb):
        return (key, ref, ref, link, kb)

    per = NSTEP // NQ // 4
    kept = {}

    def wait_barrier():
        pl.semaphore_wait(barrier, len(peers))

    task("bar", wait_barrier, after=["bin%d" % (per - 1)], cost=0.1)
    PK = FR * PB * 2 / 1024.0
    for n in range(NSTEP):
        task("bin%d" % n, functools.partial(bin_step, n), after=["bin%d" % (n - 1)] if n else [], cost=0.42)

    def keep_local(name, src, dst):
        kept[name] = local(src, dst)

    for q in range(NQ):
        for i, d in enumerate(PARTS):
            last = min((q * 4 + i + 1) * per, NSTEP - 1)
            after = ["bin%d" % last, "bar"]
            src, dst = rows_of(q, wrap(z, d)), tz.at[q, z]
            name = "z%d.%d" % (q, d)
            if d == 0:
                task(name, functools.partial(keep_local, name, src, dst), after=after, cost=0.03, prio=3)
            else:
                link = ("", "z+", "z2", "z-")[d]
                task(name, after=after, sends=[snd(name, src, dst, link, PK)], prio=3)

        here = pat.at[
            q // QC, y, c, x, pl.ds(pl.multiple_of((q % QC) * 4 * FR + z * FR, FR), FR), :
        ]

        def start_own(q=q, here=here):
            kept["z%d.0" % q].wait()
            kept["x%d" % q] = local(tz.at[q, x], here)

        group("zg%d" % q, ["z%d.%d" % (q, d) for d in (2, 1, 3)], tz.at[q, 0:3])
        group("xg%d" % q, ["x%d.%d" % (q, d) for d in (2, 1, 3)], tz.at[q, 0:3])
        task(
            "x%d" % q, start_own, waits=["zg%d" % q], after=["z%d.0" % q],
            sends=[
                snd("x%d.%d" % (q, d), tz.at[q, wrap(x, d)], here, ("", "x+", "x2", "x-")[d], PK)
                for d in (2, 1, 3)
            ], prio=3, cost=0.03,
        )

    A, B = 0, 2
    offs = (0, 3, 1, 2)

    def cast(q):
        def nm(t, *ids):
            return t + str(q) + "".join("." + str(i) for i in ids)

        ra, rb = piece(q, y, z, A, 2), piece(q, y, z, B, 2)
        task(
            nm("s"), lambda: kept["x%d" % q].wait(), waits=["xg%d" % q],
            after=["x%d" % q],
            sends=[
                same(nm("a1", 0), ra, "y+", 2 * PK), same(nm("a1", 1), ra, "y-", 2 * PK),
                same(nm("b1", 0), rb, "z+", 2 * PK), same(nm("b1", 1), rb, "z-", 2 * PK),
                same(nm("a3", 0, 0), ra, "z+", 2 * PK), same(nm("a3", 0, 1), ra, "z-", 2 * PK),
                same(nm("b3", 0, 0), rb, "y+", 2 * PK), same(nm("b3", 0, 1), rb, "y-", 2 * PK),
                same(nm("p", 0), piece(q, y, z, A, 4), "pc", 4 * PK),
            ], prio=2,
        )
        for h, (fy, fz) in enumerate((("y+", "z+"), ("y-", "z-"))):
            d = offs[h + 1]
            r, p = piece(q, wrap(y, d), z, A, 2), piece(q, wrap(y, d), z, A + h, 1)
            task(
                nm("ha", h), waits=[nm("a1", h)],
                sends=[
                    same(nm("a2", h), p, fy, PK),
                    same(nm("a3", h + 1, 0), r, "z+", 2 * PK), same(nm("a3", h + 1, 1), r, "z-", 2 * PK),
                    same(nm("p", 1 + h), r, "pc", 2 * PK),
                ], prio=2,
            )
            r, p = piece(q, y, wrap(z, d), B, 2), piece(q, y, wrap(z, d), B + h, 1)
            task(
                nm("hb", h), waits=[nm("b1", h)],
                sends=[
                    same(nm("b2", h), p, fz, PK),
                    same(nm("b3", h + 1, 0), r, "y+", 2 * PK), same(nm("b3", h + 1, 1), r, "y-", 2 * PK),
                    same(nm("p", 3 + h), r, "pc", 2 * PK),
                ], prio=2,
            )
        r = piece(q, wrap(y, 2), z, A, 2)
        group(nm("a2"), [nm("a2", 0), nm("a2", 1)], r)
        task(
            nm("ia"), waits=[nm("a2")],
            sends=[
                same(nm("a3", 3, 0), r, "z+", 2 * PK), same(nm("a3", 3, 1), r, "z-", 2 * PK),
                same(nm("p", 5), r, "pc", 2 * PK),
            ], prio=2,
        )
        r = piece(q, y, wrap(z, 2), B, 2)
        group(nm("b2"), [nm("b2", 0), nm("b2", 1)], r)
        task(
            nm("ib"), waits=[nm("b2")],
            sends=[
                same(nm("b3", 3, 0), r, "y+", 2 * PK), same(nm("b3", 3, 1), r, "y-", 2 * PK),
                same(nm("p", 6), r, "pc", 2 * PK),
            ], prio=2,
        )

        def column(zz):
            row = pl.multiple_of((q % QC) * 4 * FR + zz * FR, FR)
            return pat.at[q // QC, :, c, pl.ds(A, 2), pl.ds(row, FR), :]

        def line(yy):
            return pat.at[q // QC, yy, c, pl.ds(B, 2), pl.ds((q % QC) * 4 * FR, 4 * FR), :]

        for h, (fy, fz) in enumerate((("y+", "z+"), ("y-", "z-"))):
            e = offs[h + 1]
            for i in range(4):
                d = offs[i]
                task(
                    nm("ja", i, h), waits=[nm("a3", i, h)],
                    sends=[same(nm("a4", i, h), piece(q, wrap(y, d), wrap(z, e), A + h, 1), fz, PK)],
                    prio=2,
                )
                task(
                    nm("jb", i, h), waits=[nm("b3", i, h)],
                    sends=[same(nm("b4", i, h), piece(q, wrap(y, e), wrap(z, d), B + h, 1), fy, PK)],
                    prio=2,
                )
            task(
                nm("ka", h), after=[nm("ja", i, h) for i in range(4)],
                sends=[same(nm("p", 7 + h), column(wrap(z, e)), "pc", 8 * PK)], prio=1,
            )
            task(
                nm("kb", h), after=[nm("jb", i, h) for i in range(4)],
                sends=[same(nm("p", 9 + h), line(wrap(y, e)), "pc", 8 * PK)], prio=1,
            )
        group(nm("a4"), [nm("a4", i, h) for i in range(4) for h in range(2)], column(wrap(z, 2)))
        group(nm("b4"), [nm("b4", i, h) for i in range(4) for h in range(2)], line(wrap(y, 2)))
        rows = pl.ds((q % QC) * 4 * FR, 4 * FR)
        group(nm("p"), [nm("p", i) for i in range(13)], pat.at[q // QC, :, 1 - c, :, rows, :])
        task(
            nm("la"), waits=[nm("a4")],
            sends=[same(nm("p", 11), column(wrap(z, 2)), "pc", 8 * PK)], prio=2,
        )
        task(
            nm("lb"), waits=[nm("b4")],
            sends=[same(nm("p", 12), line(wrap(y, 2)), "pc", 8 * PK)], prio=2,
        )
        task(nm("done"), waits=[nm("p")], after=[nm("la"), nm("lb")], prio=5)

    for q in range(NQ):
        cast(q)

    def log_block(i):
        if i == 0:
            kept["tomo"].wait()
        cols = slice(i * PB, (i + 1) * PB)
        logt[:, cols] = jnp.log(tomo[:, cols].astype(F32)).astype(BF16)

    for i in range(8):
        task(
            "log%d" % i, functools.partial(log_block, i),
            after=["log%d" % (i - 1)] if i else ["bin%d" % (NSTEP - 1)], cost=0.35,
        )

    HR = NR // 2

    def lanes(d):
        return pl.ds(pl.multiple_of(wrap(x, d) * FC, FC), FC)

    infos = {}

    def slot_info(k):
        lane = lax.broadcasted_iota(jnp.int32, (NT, FC), 1)
        frame = (lane % (4 * FR)) // FR * (NF // 4) + (k * QC + lane // (4 * FR)) * FR + lane % FR
        train_of = frame // NC
        row = lax.broadcasted_iota(jnp.int32, (NT, FC), 0)
        pick = (row == train_of).astype(F32)
        ahead = (row < train_of).astype(F32)
        count = count_ref[...].astype(F32)
        group = group_ref[...].astype(F32)
        by_group = [jnp.where(group == float(g), count, 0.0) for g in range(FX)]
        weights = jnp.concatenate(by_group + [count, group, count, group], axis=0)

        def mul(m):
            return lax.dot_general(
                weights, m, (((1,), (0,)), ((), ())),
                preferred_element_type=F32, precision=lax.Precision.HIGHEST,
            )

        here, before = mul(pick), mul(ahead)
        own_group = here[5:6]
        slot = (frame[0:1] % NC).astype(F32)
        live = (slot < here[4:5]).astype(F32)
        place = slot
        for g in range(FX):
            place = place + jnp.where(own_group == float(g), before[g:g + 1], 0.0)
        infos[k] = (live, jnp.where(live > 0.0, place, -1.0), own_group)

    loglik = {}

    def scores_chain(k):
        def nm(t, *ids):
            return t + "k" + str(k) + "".join("." + str(i) for i in ids)

        task(nm("info"), functools.partial(slot_info, k), after=["bin%d" % (NSTEP - 1)], cost=0.5, prio=-1)

        def dots():
            total = None
            for yy in range(4):
                for cc in range(2):
                    blk = yy * 2 + cc
                    part = lax.dot_general(
                        logt[:, blk * PB:(blk + 1) * PB],
                        pat[k, yy, cc].reshape(FX * FC, PB),
                        (((1,), (1,)), ((), ())),
                        preferred_element_type=F32,
                    )
                    total = part if total is None else total + part
            sall[k] = total

        SK = HR * FC * 4 / 1024.0
        task(
            nm("dots"), dots, after=["done%d" % (k * QC + i) for i in range(QC)] + ["log7"], cost=0.8, prio=1,
            sends=[
                snd(nm("far", 0), sall.at[k, 0:HR, lanes(2)], far.at[k, 0], "x+", SK),
                snd(nm("far", 1), sall.at[k, HR:NR, lanes(2)], far.at[k, 1], "x-", SK),
                snd(nm("near", 0), sall.at[k, HR:NR, lanes(1)], near.at[k, 0, HR:NR], "x+", SK),
                snd(nm("near", 1), sall.at[k, 0:HR, lanes(3)], near.at[k, 1, 0:HR], "x-", SK),
            ],
        )

        def add(h):
            rows, d = ((slice(0, HR), 1), (slice(HR, NR), 3))[h]
            own[k, h] = sall[k, rows, lanes(d)] + far[k, h]

        task(
            nm("add", 0), functools.partial(add, 0), waits=[nm("far", 0)], cost=0.05, prio=2,
            sends=[snd(nm("near", 2), own.at[k, 0], near.at[k, 0, 0:HR], "x+", SK)],
        )
        task(
            nm("add", 1), functools.partial(add, 1), waits=[nm("far", 1)], cost=0.05, prio=2,
            sends=[snd(nm("near", 3), own.at[k, 1], near.at[k, 1, HR:NR], "x-", SK)],
        )

        def stats1():
            scores = (sall[k, :, lanes(0)] + near[k, 0] + near[k, 1]) * SCALE
            high = jnp.max(scores, axis=0, keepdims=True)
            weights = jnp.exp(scores - high)
            wexp[k] = weights
            mine = staty.at[k, y * 2 + c]
            mine[0:1, :] = high
            mine[1:2, :] = jnp.sum(weights, axis=0, keepdims=True)
            high_s[k] = high

        group(nm("near"), [nm("near", i) for i in range(4)], near.at[k])
        group(nm("sy"), [nm("sy", d, f) for d in range(4) for f in range(2) if d or f], staty.at[k, 0:7])
        group(nm("sz"), [nm("sz", d) for d in (1, 2, 3)], statz.at[k, 0:3])
        group(nm("r2"), [nm("r2", 0), nm("r2", 1)], resp.at[k, :, lanes(2)])
        mine = staty.at[k, y * 2 + c]
        task(
            nm("st1"), stats1, waits=[nm("near")], cost=0.3, prio=2,
            sends=[
                snd(nm("sy", d, f), mine, mine, dev(dy=d, flip=bool(f)), 1.0)
                for d in range(4) for f in range(2) if d or f
            ],
        )

        def merge(ref):
            highs, sums = ref[k, :, 0, :], ref[k, :, 1, :]
            high = jnp.max(highs, axis=0, keepdims=True)
            return high, jnp.sum(sums * jnp.exp(highs - high), axis=0, keepdims=True)

        def stats2():
            high, total = merge(staty)
            mine = statz.at[k, z]
            mine[0:1, :] = high
            mine[1:2, :] = total

        minez = statz.at[k, z]
        task(
            nm("st2"), stats2, cost=0.1, prio=2,
            waits=[nm("sy")],
            sends=[snd(nm("sz", d), minez, minez, dev(dz=d), 1.0) for d in (2, 1, 3)],
        )

        def stats3():
            live = infos[k][0]
            highest, partition = merge(statz)
            factor = jnp.exp(high_s[k] - highest) / partition * live
            resp[k, :, lanes(0)] = (wexp[k] * factor).astype(BF16)
            loglik[k] = (highest + jnp.log(partition)) * live

        RK = NR * FC * 2 / 1024.0
        r = resp.at[k, :, lanes(0)]
        task(
            nm("st3"), stats3, waits=[nm("sz")], after=[nm("info")], cost=0.3, prio=2,
            sends=[same(nm("r1", 0), r, "x+", RK), same(nm("r1", 1), r, "x-", RK)],
        )
        task(
            nm("g", 0), waits=[nm("r1", 0)], prio=2,
            sends=[same(nm("r2", 0), resp.at[k, 0:HR, lanes(3)], "x+", RK / 2)],
        )
        task(
            nm("g", 1), waits=[nm("r1", 1)], prio=2,
            sends=[same(nm("r2", 1), resp.at[k, HR:NR, lanes(1)], "x-", RK / 2)],
        )

    for k in range(KC):
        scores_chain(k)

    def place_loglik():
        for g in range(FX):
            total = None
            for k in range(KC):
                _, place, own_group = infos[k]
                slot = lax.broadcasted_iota(jnp.int32, (NF // FX, FC), 0).astype(F32)
                mask = ((slot == place) & (own_group == float(g))).astype(F32)
                part = lax.dot_general(
                    jnp.broadcast_to(loglik[k], (8, FC)), mask, (((1,), (1,)), ((), ())),
                    preferred_element_type=F32, precision=lax.Precision.HIGHEST,
                )
                total = part if total is None else total + part
            llsend[g] = total
        llrecv[x] = llsend[x]

    task(
        "ll", place_loglik, after=["st3k%d" % k for k in range(KC)], cost=0.4, prio=1,
        sends=[snd("ll.%d" % d, llsend.at[wrap(x, d)], llrecv.at[x], dev(dx=d), 2.0) for d in (2, 1, 3)],
    )
    group("llg", ["ll.%d" % d for d in (1, 2, 3)], llrecv.at[0:3])

    def part_of_numerator(i):
        total = None
        for k in range(KC - 1):
            part = jnp.dot(
                resp[k], pat[k, i // 2, i % 2].reshape(FX * FC, PB), preferred_element_type=F32
            )
            total = part if total is None else total + part
        num[:, i * PB:(i + 1) * PB] = total

    for i in range(8):
        before = ["num%d" % (i - 1)] if i else ["gk%d.%d" % (KC - 2, h) for h in range(2)]
        waits = [] if i else ["r2k%d" % k for k in range(KC - 1)]
        task("num%d" % i, functools.partial(part_of_numerator, i), waits=waits, after=before, cost=0.35)
    task(
        "end", waits=["llg", "r2k%d" % (KC - 1)],
        after=["gk%d.%d" % (KC - 1, h) for h in range(2)] + ["num7"],
    )

    for name, fn, waits, _, sends, _, _ in in_order(tasks, groups):
        for w in waits:
            await_arrival(w)
        if fn is not None:
            fn()
        for key, src, dst, link, _ in sends:
            remote(key, src, dst, LINKS[link] if isinstance(link, str) else link)
    for d in started[-N_SEND:]:
        d.wait_send()


def in_order(tasks, groups, show=False):
    per_kb = 1024.0 / 60.0e3
    free, came, when = {}, {}, {}
    left = list(tasks)
    out = []
    t = 1.5

    def members(names):
        return [key for w in names for key in (groups[w][0] if w in groups else (w,))]

    while left:
        best = None
        for i, (name, _, waits, after, sends, cost, prio) in enumerate(left):
            keys = members(waits)
            if any(a not in when for a in after) or any(w not in came for w in keys):
                continue
            ready = max([came[w] for w in keys] + [t])
            if name.startswith("bin"):
                ready = max(ready, 2.6 + 0.36 * int(name[3:]))
            if name[0] == "s" and name[1].isdigit():
                ready = max([ready] + [free.get(v[3], 0.0) - BACKLOG for v in sends])
            rank = (ready > t, ready if ready > t else 0.0, -prio, ready)
            if best is None or rank < best[0]:
                best = (rank, i, ready)
        _, i, ready = best
        item = left.pop(i)
        name, _, waits, _, sends, cost, _ = item
        t = ready + cost + 0.02 * len(waits)
        for key, _, _, link, kb in sends:
            t += 0.012
            if not isinstance(link, str):
                came[key] = t + 2.6
                continue
            hops = {"pc": 0}.get(link, 2 if link[1] == "2" else 1)
            lane = link[0] + "+" if hops == 2 else link
            busy = kb * 1024.0 / 500e3 if link == "pc" else kb * per_kb * hops
            start = max(t, free.get(lane, 0.0))
            free[lane] = start + busy
            came[key] = start + busy + (0.9, 1.7, 2.5)[hops]
        when[name] = t
        out.append(item)
        if show:
            print("%7.2f %s" % (t, name))
    return out


BACKLOG = 8.0
N_SEND = 24
N_RECV = 125
N_LOCAL = 16


def exchange(raw, off, gain, sec, cell, tomograms, count, group):
    vmem = pl.BlockSpec(memory_space=pltpu.VMEM)
    any_ = pl.BlockSpec(memory_space=pltpu.HBM)
    return pl.pallas_call(
        comm_kernel,
        in_specs=[any_] * 9,
        out_specs=[vmem] * 5,
        out_shape=[
            pltpu.VMEM((KC, 4, 2, FX, FC, PB), BF16),
            pltpu.VMEM((KC, NR, FX * FC), BF16),
            pltpu.VMEM((NR, SLICE), BF16),
            pltpu.VMEM((NR, SLICE), F32),
            pltpu.VMEM((FX, 8, NF // FX), F32),
        ],
        scratch_shapes=[
            pltpu.VMEM((NBUF, BT, NC, PIXSUB, PB), BF16),
            pltpu.VMEM((3, NC, PIXSUB, PB), BF16),
            pltpu.VMEM((3, NC, PIXSUB, PB), BF16),
            pltpu.VMEM((NC, PIXSUB, PB), jnp.int32),
            pltpu.VMEM((NC, PIXSUB, PB), F32),
            pltpu.VMEM((NC, 8, PB), F32),
            pltpu.VMEM((PB // 128, BT * NC * 8, 128), F32),
            pltpu.VMEM((NF, PB), BF16),
            pltpu.VMEM((NQ, 4, FR, PB), BF16),
            pltpu.VMEM((NR, SLICE), BF16),
            pltpu.VMEM((KC, NR, FX * FC), F32),
            pltpu.VMEM((KC, 2, NR // 2, FC), F32),
            pltpu.VMEM((KC, 2, NR, FC), F32),
            pltpu.VMEM((KC, 2, NR // 2, FC), F32),
            pltpu.VMEM((KC, NR, FC), F32),
            pltpu.VMEM((KC, 1, FC), F32),
            pltpu.VMEM((KC, 8, 2, FC), F32),
            pltpu.VMEM((KC, 4, 2, FC), F32),
            pltpu.VMEM((FX, 8, NF // FX), F32),
            pltpu.SMEM((NC, NT), jnp.int32),
            pltpu.SMEM((NT,), jnp.int32),
            pltpu.VMEM((1, NT), jnp.int32),
            pltpu.VMEM((1, NT), jnp.int32),
            pltpu.SemaphoreType.DMA((N_SEND,)),
            pltpu.SemaphoreType.DMA((N_RECV,)),
            pltpu.SemaphoreType.DMA((N_LOCAL,)),
            pltpu.SemaphoreType.DMA((NBUF,)),
        ],
        compiler_params=pltpu.CompilerParams(
            collective_id=0, has_side_effects=True, vmem_limit_bytes=45 << 20
        ),
        name="exchange",
    )(cell.T, count, raw, off, gain, sec, tomograms, count.reshape(1, NT), group.reshape(1, NT))


WIDE = 4


def update_kernel(pat_ref, resp_ref, tomo_ref, num_ref, ll_ref, out_ref, llo_ref, inv_s):
    step = pl.program_id(0)

    @pl.when(step == 0)
    def _():
        total = None
        for k in range(KC):
            part = jnp.sum(resp_ref[k].astype(F32), axis=1, keepdims=True)
            total = part if total is None else total + part
        inv_s[...] = 1.0 / (total + SMOOTHING)
        llo_ref[...] = jnp.concatenate([ll_ref[b, 0:1, :] for b in range(FX)], axis=1)

    for h in range(WIDE):
        block = step * WIDE + h
        columns = pl.ds(pl.multiple_of(block * PB, PB), PB)
        total = num_ref[:, columns] + jnp.dot(
            resp_ref[KC - 1], pat_ref[KC - 1, block // 2, block % 2].reshape(FX * FC, PB),
            preferred_element_type=F32,
        )
        total = total + SMOOTHING * tomo_ref[:, columns].astype(F32)
        out_ref[:, h * PB:(h + 1) * PB] = total * inv_s[...]


def update(pat, resp, tomo, num, ll):
    vmem = pl.BlockSpec(memory_space=pltpu.VMEM)
    return pl.pallas_call(
        update_kernel,
        grid=(8 // WIDE,),
        in_specs=[vmem] * 5,
        out_specs=[
            pl.BlockSpec((NR, WIDE * PB), lambda i: (0, i)),
            pl.BlockSpec((1, NF), lambda i: (0, 0)),
        ],
        out_shape=[
            jax.ShapeDtypeStruct((NR, SLICE), F32),
            jax.ShapeDtypeStruct((1, NF), F32),
        ],
        scratch_shapes=[pltpu.VMEM((NR, 1), F32)],
        compiler_params=pltpu.CompilerParams(vmem_limit_bytes=24 << 20),
        name="update",
    )(pat, resp, tomo, num, ll)


def on_device(
    raw_frames, offset_table, gain_table, gain_section, hit_cell, hit_count, train_group, tomograms
):
    pat, resp, tomo, num, ll = exchange(
        raw_frames, offset_table, gain_table, gain_section, hit_cell, tomograms,
        hit_count, train_group,
    )
    new_tomograms, loglik = update(pat, resp, tomo, num, ll)
    return new_tomograms, loglik.reshape(NF)


def solution(mesh):
    placed = (
        P("frames", None, None, "orient"),
        P(None, None, None, "orient"),
        P(None, None, None, "orient"),
        P(None, None, "orient"),
        P("frames", None),
        P("frames"),
        P("frames"),
        P("orient", None),
    )
    return jax.shard_map(
        on_device,
        mesh=mesh,
        in_specs=placed,
        out_specs=(P("orient", "frames"), P("frames")),
        check_vma=False,
    )
```
